256 devices in a mesh: seq: 16 (over y, x), chan: 16 (over z, core).
Axes of the slice: x: 4, y: 4, z: 8, core: 2. Of those that a mesh axis runs over, the one named last changes fastest.
Arguments:
- signal: float32 [8192, 4096], P('seq', 'chan'), may hold values from -6 to 6
- filter_taps: float32 [8192, 4096], P('seq', 'chan'), may hold values from -3 to 3
- out_gate: float32 [8192, 4096], P('seq', 'chan'), may hold values from -6 to 6
- skip_gain: float32 [4096], P('chan'), may hold values from -4 to 4
- lengths: int32 [128], replicated, may hold values from 1 to 512, 8192 in all
- row_of_segment: int32 [128], replicated, may hold values from 0 to 127, each once
Outputs:
- mixed: float32 [8192, 4096], P('seq', 'chan')
- pooled: float32 [128, 4096], P('seq', 'chan')
The draws below stay inside these ranges and needn't reach their ends.
Inputs may be any that keep to these rules, and one draw needn't show every extreme that they name: `lengths`: segments tile the sequence; pooled row r belongs to index r // 8 of seq. `row_of_segment`: each row appears once.
All inputs are finite; a program needn't handle non-finite values.
Results may differ from the reference program's by a relative error of at most 0.000078.
Values sent between devices are 32-bit elements; how exact they have to be, the bound alone decides.
No kernel may reach another device: no remote copies, remote signals or barrier semaphores. Data moves between devices by JAX's collectives and lax.ppermute only.
A program may use at most 64 MiB of HBM per device.

```python
import math
import jax
import jax.numpy as jnp
import numpy as np
from jax import lax

D = 4096
TOK_DEV = 512
TOKENS = 8192
SEGS = 128


def draw_filter_taps(key, part):
    key_decay, key_values = jax.random.split(key)
    low_end = math.log(20.0)
    decay_len = jnp.exp(jax.random.uniform(key_decay, (D,), jnp.float32, low_end, math.log(4.0 * TOKENS)))
    noise_part = jnp.clip(jax.random.normal(key_values, (TOKENS, D), jnp.float32), -6.0, 6.0)
    places = jnp.arange(TOKENS, dtype=jnp.float32)[:, None]
    envelope = jnp.exp(-places / decay_len[None, :]) * jnp.sqrt(2.0 / decay_len)[None, :]
    return noise_part * envelope


def block_levels(own_key, dims, cuts, low, high):
    gain, own = 1.0, jax.random.fold_in(own_key, 6)
    for axis_at, blocks in cuts:
        steps = jnp.exp(jax.random.uniform(jax.random.fold_in(own, axis_at), (blocks,), jnp.float32, low / len(cuts), high / len(cuts)))
        gain = gain * jnp.repeat(steps, dims[axis_at] // blocks).reshape([-1 if axis == axis_at else 1 for axis in range(len(dims))])
    return gain


def split_up(amount, total, most, skew):
    portions = [(1 << 20) // math.isqrt(grade ** skew) + 1 for grade in range(2, amount + 1)]
    spare, holding = total - most - (amount - 1), [1] * (amount - 1)
    while spare > 0:
        candidates = [i for i in range(amount - 1) if holding[i] < most]
        whole, remaining = sum([portions[i] for i in candidates]), spare
        for i in candidates:
            more = min(most - holding[i], max(1, remaining * portions[i] // whole), spare)
            holding[i] = holding[i] + more
            spare = spare - more
    return np.array([most] + holding)


def uneven(key, amount, total, reach, lean):
    if amount == 2:
        one = jax.random.randint(key, (), max(1, total - reach), min(reach, total - 1) + 1)
        return jnp.stack([one, total - one])
    sizes = jnp.asarray(split_up(amount, total, reach, lean), jnp.int32)
    pairs = (amount - 1) // 2
    donor, sink = sizes[1:1 + 2 * pairs:2], sizes[2:2 + 2 * pairs:2]
    room = jnp.minimum(donor - 1, reach - sink)
    passed = jax.random.randint(jax.random.fold_in(key, 1), (pairs,), 0, 1 << 20) % (room + 1)
    sizes = sizes.at[1:1 + 2 * pairs:2].set(donor - passed).at[2:2 + 2 * pairs:2].set(sink + passed)
    return sizes[jax.random.permutation(jax.random.fold_in(key, 2), amount)]


def scatter_about(key, shape, deviation, reach, pieces=(), held_as=jnp.bfloat16):
    drawn = deviation * jax.random.normal(key, shape, jnp.float32)
    if pieces:
        drawn = drawn * block_levels(key, shape, pieces, -0.22, 0.18)
    return jnp.clip(drawn, -reach, reach).astype(held_as)


def setup_inputs(seed: int = 0) -> dict:
    key_of = jax.random.split(jax.random.key(seed), 7)
    return {
        "signal": scatter_about(key_of[0], (TOKENS, D), 1.0, 6.0, ((0, 16), (1, 16)), jnp.float32),
        "filter_taps": draw_filter_taps(jax.random.fold_in(key_of[6], 71), 0),
        "out_gate": scatter_about(key_of[2], (TOKENS, D), 1.0, 6.0, ((0, 16), (1, 16)), jnp.float32),
        "skip_gain": scatter_about(key_of[3], (D,), 1.0, 4.0, ((0, 16),), jnp.float32),
        "lengths": uneven(key_of[4], SEGS, TOKENS, TOK_DEV, 2).astype(jnp.int32),
        "row_of_segment": jax.random.permutation(key_of[5], SEGS).astype(jnp.int32),
    }


def convolve_block(pair):
    signal_block, taps_block = pair
    signal_spec = jnp.fft.rfft(signal_block, n=2 * TOKENS, axis=0)
    taps_spec = jnp.fft.rfft(taps_block, n=2 * TOKENS, axis=0)
    return jnp.fft.irfft(signal_spec * taps_spec, n=2 * TOKENS, axis=0)[:TOKENS]


def reference(signal, filter_taps, out_gate, skip_gain, lengths, row_of_segment):
    block_width = min(256, D)
    groups = D // block_width
    signal_blocks = jnp.transpose(signal.reshape(TOKENS, groups, block_width), (1, 0, 2))
    taps_blocks = jnp.transpose(filter_taps.reshape(TOKENS, groups, block_width), (1, 0, 2))
    conv_blocks = lax.map(convolve_block, (signal_blocks, taps_blocks))
    conv = jnp.transpose(conv_blocks, (1, 0, 2)).reshape(TOKENS, D).astype(signal.dtype)
    mixed = out_gate * (conv + skip_gain[None, :] * signal)
    segment_ids = jnp.repeat(jnp.arange(SEGS, dtype=jnp.int32), lengths, total_repeat_length=TOKENS)
    sums = jax.ops.segment_sum(mixed, segment_ids, num_segments=SEGS)
    means = sums / lengths.astype(mixed.dtype)[:, None]
    pooled = jnp.zeros_like(means).at[row_of_segment].set(means)
    return mixed, pooled
```

```python
import functools
import math

import jax
import jax.numpy as jnp
import numpy as np
from jax import lax
from jax.experimental import pallas as pl
from jax.experimental.pallas import tpu as pltpu
from jax.sharding import PartitionSpec as P


LANES = 128
INTERPRET = False
bf16 = jnp.bfloat16
f32 = jnp.float32


def split_const(value):
    hi = value.astype(bf16)
    return hi, (value - hi.astype(np.float64)).astype(bf16)


@functools.lru_cache(None)
def tables(seq_count, subs):
    rows = seq_count * subs
    total = rows * LANES
    t1 = np.array([device * subs + sub for sub in range(subs) for device in range(seq_count)], np.float64)
    k1 = np.arange(rows, dtype=np.float64)
    t2 = np.arange(LANES, dtype=np.float64)
    first = -2.0 * math.pi * (k1[:, None] + 0.25) * t1[None, :] / rows
    first = np.concatenate([np.cos(first), np.sin(first)], 0)
    hi, lo = split_const(first)
    first3 = np.concatenate([hi, lo, hi], 1)
    twist = -2.0 * math.pi * (k1[:, None] + 0.25) * t2[None, :] / total
    twist = np.stack([np.cos(twist), np.sin(twist)]).astype(np.float32)
    angle = 2.0 * math.pi * (np.outer(t2, t2) % LANES) / LANES
    cos, sin = np.cos(angle), np.sin(angle)
    forward = np.block([[cos, -sin], [sin, cos]])
    hi, lo = split_const(forward)
    forward3 = np.concatenate([hi, hi, lo], 0)
    hi, lo = split_const(forward.T / total)
    inverse3 = np.concatenate([hi, hi, lo], 0)
    last = 2.0 * math.pi * t1[:, None] * (k1[None, :] + 0.25) / rows
    hi, lo = split_const(np.concatenate([np.cos(last), -np.sin(last)], 1))
    last3 = np.concatenate([hi, lo, hi], 1)
    return first3, twist, forward3, inverse3, last3


def split(value):
    hi = value.astype(bf16)
    lo = (value - hi.astype(f32)).astype(bf16)
    return hi, lo


def mm(left, right):
    return lax.dot_general(left, right, (((1,), (0,)), ((), ())), preferred_element_type=f32)


def turn_kernel(signal, taps, gate, skip, out, *, seq_count, group, subs):
    at_start = lax.axis_index("seq") == 0
    for sub in range(subs):
        rows = slice(sub * LANES, (sub + 1) * LANES)
        for which, ref in enumerate((signal, taps, gate)):
            value = ref[rows, :]
            if which == 1 and sub == 0:
                place = lax.broadcasted_iota(jnp.int32, value.shape, 0)
                value = value + jnp.where((place == 0) & at_start, skip[...], 0.0)
            base = (sub * 3 + which) * group
            out[:, base : base + group, :] = value.T.reshape(seq_count, group, LANES)


def conv_kernel(
    taken, lengths, row_of, first3, twist, forward3, inverse3, last3, out, conv, *, seq_count, group, subs
):
    rows = seq_count * subs
    per = 3 * subs * group
    twist_re, twist_im = twist[0], twist[1]
    pair = 2

    def gather(which, channel):
        parts = []
        for sub in range(subs):
            start = (sub * 3 + which) * group + channel
            parts.append(taken[pl.ds(start, seq_count, stride=per), :])
        return jnp.concatenate(parts, 0)

    for block in range(group // pair):
        turned = []
        for channel in range(block * pair, (block + 1) * pair):
            both = jnp.concatenate([gather(0, channel), gather(1, channel)], 1)
            hi, lo = split(both)
            stage = mm(first3[...], jnp.concatenate([hi, hi, lo], 0))
            for side in range(2):
                lanes = slice(side * LANES, (side + 1) * LANES)
                re, im = stage[:rows, lanes], stage[rows:, lanes]
                turned.append(
                    jnp.concatenate([re * twist_re - im * twist_im, re * twist_im + im * twist_re], 1)
                )
        hi, lo = split(jnp.concatenate(turned, 0))
        spec = mm(jnp.concatenate([hi, lo, hi], 1), forward3[...])
        products = []
        for at in range(pair):
            left = spec[(2 * at) * rows : (2 * at + 1) * rows]
            right = spec[(2 * at + 1) * rows : (2 * at + 2) * rows]
            left_re, left_im = left[:, :LANES], left[:, LANES:]
            right_re, right_im = right[:, :LANES], right[:, LANES:]
            products.append(
                jnp.concatenate(
                    [left_re * right_re - left_im * right_im, left_re * right_im + left_im * right_re], 1
                )
            )
        hi, lo = split(jnp.concatenate(products, 0))
        back = mm(jnp.concatenate([hi, lo, hi], 1), inverse3[...])
        untwisted = []
        for at in range(pair):
            re, im = back[at * rows : (at + 1) * rows, :LANES], back[at * rows : (at + 1) * rows, LANES:]
            untwisted.append(
                jnp.concatenate([re * twist_re + im * twist_im, im * twist_re - re * twist_im], 0)
            )
        hi, lo = split(jnp.concatenate(untwisted, 1))
        result = mm(last3[...], jnp.concatenate([hi, hi, lo], 0))
        for at in range(pair):
            channel = block * pair + at
            for sub in range(subs):
                conv[pl.ds(sub * group + channel, seq_count, stride=subs * group), :] = result[
                    sub * seq_count : (sub + 1) * seq_count, at * LANES : (at + 1) * LANES
                ]

    segs = lengths.shape[1]
    owned = segs // seq_count
    seg_len = lengths[...].astype(f32)
    seg_at = lax.broadcasted_iota(jnp.int32, (segs, segs), 1)
    hit = row_of[...] == lax.broadcasted_iota(jnp.int32, (segs, segs), 0)
    which_seg = jnp.sum(jnp.where(hit, seg_at, 0).astype(f32), axis=1, keepdims=True)
    row_len = jnp.sum(jnp.where(hit, seg_len, 0.0), axis=1, keepdims=True)
    row_start = jnp.sum(jnp.where(seg_at.astype(f32) < which_seg, seg_len, 0.0), axis=1, keepdims=True)
    row_end = row_start + row_len
    token = lax.broadcasted_iota(jnp.int32, (segs, 2 * LANES), 1).astype(f32)
    acc = jnp.zeros((segs, 2 * group), f32)
    for device in range(seq_count):
        for step in range(subs // 2):
            halves = []
            for sub in (2 * step, 2 * step + 1):
                base = (device * subs + sub) * group
                from_row = device * per + (sub * 3 + 2) * group
                mixed = conv[base : base + group, :] * taken[from_row : from_row + group, :]
                out[device, sub * group : (sub + 1) * group, :] = mixed
                halves.append(mixed)
            hi, lo = split(jnp.concatenate(halves, 1))
            here = token + float((device * subs + 2 * step) * LANES)
            member = jnp.where((here >= row_start) & (here < row_end), 1.0, 0.0).astype(bf16)
            acc = acc + lax.dot_general(
                member,
                jnp.concatenate([hi, lo], 0),
                (((1,), (1,)), ((), ())),
                preferred_element_type=f32,
            )
    pooled = (acc[:, :group] + acc[:, group:]) / row_len
    pooled = jnp.concatenate([pooled, jnp.zeros((segs, LANES - group), f32)], 1)
    shift = lax.rem(lax.axis_index("seq"), LANES // group) * group
    pooled = pltpu.roll(pooled, shift, 1)
    out[:, subs * group :, :] = pooled.reshape(seq_count, owned, LANES)


def back_kernel(taken, mixed, pooled, *, seq_count, group, subs):
    channels = seq_count * group
    for sub in range(subs):
        block = taken[:, sub * group : (sub + 1) * group, :].reshape(channels, LANES)
        mixed[sub * LANES : (sub + 1) * LANES, :] = block.T
    per_lane = LANES // group
    for half in range(channels // LANES):
        total = taken[half * per_lane, subs * group :, :]
        for at in range(half * per_lane + 1, (half + 1) * per_lane):
            total = total + taken[at, subs * group :, :]
        pooled[:, half * LANES : (half + 1) * LANES] = total


def on_device(signal, filter_taps, out_gate, skip_gain, lengths, row_of_segment):
    seq_count = lax.axis_size("seq")
    block_rows, channels = signal.shape
    group = channels // seq_count
    subs = block_rows // LANES
    segs = lengths.shape[0]
    owned = segs // seq_count
    sizes = dict(seq_count=seq_count, group=group, subs=subs)
    sent = pl.pallas_call(
        functools.partial(turn_kernel, **sizes),
        out_shape=jax.ShapeDtypeStruct((seq_count, 3 * subs * group, LANES), f32),
        interpret=INTERPRET,
        name="turn",
    )(signal, filter_taps, out_gate, skip_gain.reshape(1, channels))
    taken = lax.all_to_all(sent, "seq", 0, 0)
    consts = [jnp.asarray(table) for table in tables(seq_count, subs)]
    mixed_sent = pl.pallas_call(
        functools.partial(conv_kernel, **sizes),
        out_shape=jax.ShapeDtypeStruct((seq_count, subs * group + owned, LANES), f32),
        scratch_shapes=[pltpu.VMEM((seq_count * subs * group, LANES), f32)],
        interpret=INTERPRET,
        name="conv",
    )(
        taken.reshape(seq_count * 3 * subs * group, LANES),
        lengths.reshape(1, segs),
        row_of_segment.reshape(1, segs),
        *consts,
    )
    back = lax.all_to_all(mixed_sent, "seq", 0, 0)
    return pl.pallas_call(
        functools.partial(back_kernel, **sizes),
        out_shape=(
            jax.ShapeDtypeStruct((block_rows, channels), f32),
            jax.ShapeDtypeStruct((owned, channels), f32),
        ),
        interpret=INTERPRET,
        name="back",
    )(back)


def solution(mesh):
    placed = (P("seq", "chan"), P("seq", "chan"), P("seq", "chan"), P("chan"), P(), P())
    return jax.shard_map(
        on_device,
        mesh=mesh,
        in_specs=placed,
        out_specs=(P("seq", "chan"), P("seq", "chan")),
        check_vma=False,
    )
```

```python
import functools
import math

import jax
import jax.numpy as jnp
import numpy as np
from jax import lax
from jax.experimental import pallas as pl
from jax.experimental.pallas import tpu as pltpu
from jax.sharding import PartitionSpec as P


LANES = 128
INTERPRET = False
bf16 = jnp.bfloat16
f32 = jnp.float32


def split_const(value):
    hi = value.astype(bf16)
    return hi, (value - hi.astype(np.float64)).astype(bf16)


@functools.lru_cache(None)
def tables(seq_count, subs):
    rows = seq_count * subs
    total = rows * LANES
    t1 = np.array([device * subs + sub for sub in range(subs) for device in range(seq_count)], np.float64)
    k1 = np.arange(rows, dtype=np.float64)
    t2 = np.arange(LANES, dtype=np.float64)
    first = -2.0 * math.pi * (k1[:, None] + 0.25) * t1[None, :] / rows
    first = np.concatenate([np.cos(first), np.sin(first)], 0)
    hi, lo = split_const(first)
    first3 = np.concatenate([hi, lo, hi], 1)
    twist = -2.0 * math.pi * (k1[:, None] + 0.25) * t2[None, :] / total
    twist = np.stack([np.cos(twist), np.sin(twist)]).astype(np.float32)
    angle = 2.0 * math.pi * (np.outer(t2, t2) % LANES) / LANES
    cos, sin = np.cos(angle), np.sin(angle)
    forward = np.block([[cos, -sin], [sin, cos]])
    hi, lo = split_const(forward)
    forward3 = np.concatenate([hi, hi, lo], 0)
    hi, lo = split_const(forward.T / total)
    inverse3 = np.concatenate([hi, hi, lo], 0)
    last = 2.0 * math.pi * t1[:, None] * (k1[None, :] + 0.25) / rows
    hi, lo = split_const(np.concatenate([np.cos(last), -np.sin(last)], 1))
    last3 = np.concatenate([hi, lo, hi], 1)
    return first3, twist, forward3, inverse3, last3


def split(value):
    hi = value.astype(bf16)
    lo = (value - hi.astype(f32)).astype(bf16)
    return hi, lo


def mm(left, right):
    return lax.dot_general(left, right, (((1,), (0,)), ((), ())), preferred_element_type=f32)


def turn_kernel(signal, taps, gate, skip, out, *, seq_count, group, subs):
    at_start = lax.axis_index("seq") == 0
    for sub in range(subs):
        rows = slice(sub * LANES, (sub + 1) * LANES)
        for which, ref in enumerate((signal, taps, gate)):
            value = ref[rows, :]
            if which == 1 and sub == 0:
                place = lax.broadcasted_iota(jnp.int32, value.shape, 0)
                value = value + jnp.where((place == 0) & at_start, skip[...], 0.0)
            base = (sub * 3 + which) * group
            out[:, base : base + group, :] = value.T.reshape(seq_count, group, LANES)


def conv_kernel(
    taken, lengths, row_of, first3, twist, forward3, inverse3, last3, out, conv, *, seq_count, group, subs
):
    rows = seq_count * subs
    per = 3 * subs * group
    twist_re, twist_im = twist[0], twist[1]
    pair = 2

    def gather(which, channel):
        parts = []
        for sub in range(subs):
            start = (sub * 3 + which) * group + channel
            parts.append(taken[pl.ds(start, seq_count, stride=per), :])
        return jnp.concatenate(parts, 0)

    for block in range(group // pair):
        turned = []
        for channel in range(block * pair, (block + 1) * pair):
            both = jnp.concatenate([gather(0, channel), gather(1, channel)], 1)
            hi, lo = split(both)
            stage = mm(first3[...], jnp.concatenate([hi, hi, lo], 0))
            for side in range(2):
                lanes = slice(side * LANES, (side + 1) * LANES)
                re, im = stage[:rows, lanes], stage[rows:, lanes]
                turned.append(
                    jnp.concatenate([re * twist_re - im * twist_im, re * twist_im + im * twist_re], 1)
                )
        hi, lo = split(jnp.concatenate(turned, 0))
        spec = mm(jnp.concatenate([hi, lo, hi], 1), forward3[...])
        products = []
        for at in range(pair):
            left = spec[(2 * at) * rows : (2 * at + 1) * rows]
            right = spec[(2 * at + 1) * rows : (2 * at + 2) * rows]
            left_re, left_im = left[:, :LANES], left[:, LANES:]
            right_re, right_im = right[:, :LANES], right[:, LANES:]
            products.append(
                jnp.concatenate(
                    [left_re * right_re - left_im * right_im, left_re * right_im + left_im * right_re], 1
                )
            )
        hi, lo = split(jnp.concatenate(products, 0))
        back = mm(jnp.concatenate([hi, lo, hi], 1), inverse3[...])
        untwisted = []
        for at in range(pair):
            re, im = back[at * rows : (at + 1) * rows, :LANES], back[at * rows : (at + 1) * rows, LANES:]
            untwisted.append(
                jnp.concatenate([re * twist_re + im * twist_im, im * twist_re - re * twist_im], 0)
            )
        hi, lo = split(jnp.concatenate(untwisted, 1))
        result = mm(last3[...], jnp.concatenate([hi, hi, lo], 0))
        for at in range(pair):
            channel = block * pair + at
            for sub in range(subs):
                conv[pl.ds(sub * group + channel, seq_count, stride=subs * group), :] = result[
                    sub * seq_count : (sub + 1) * seq_count, at * LANES : (at + 1) * LANES
                ]

    segs = lengths.shape[1]
    owned = segs // seq_count
    seg_len = lengths[...].astype(f32)
    seg_at = lax.broadcasted_iota(jnp.int32, (segs, segs), 1)
    hit = row_of[...] == lax.broadcasted_iota(jnp.int32, (segs, segs), 0)
    which_seg = jnp.sum(jnp.where(hit, seg_at, 0).astype(f32), axis=1, keepdims=True)
    row_len = jnp.sum(jnp.where(hit, seg_len, 0.0), axis=1, keepdims=True)
    row_start = jnp.sum(jnp.where(seg_at.astype(f32) < which_seg, seg_len, 0.0), axis=1, keepdims=True)
    row_end = row_start + row_len
    token = lax.broadcasted_iota(jnp.int32, (segs, 2 * LANES), 1).astype(f32)
    acc = jnp.zeros((segs, 2 * group), f32)
    for device in range(seq_count):
        for step in range(subs // 2):
            halves = []
            for sub in (2 * step, 2 * step + 1):
                base = (device * subs + sub) * group
                from_row = device * per + (sub * 3 + 2) * group
                mixed = conv[base : base + group, :] * taken[from_row : from_row + group, :]
                out[device, sub * group : (sub + 1) * group, :] = mixed
                halves.append(mixed)
            hi, lo = split(jnp.concatenate(halves, 1))
            here = token + float((device * subs + 2 * step) * LANES)
            member = jnp.where((here >= row_start) & (here < row_end), 1.0, 0.0).astype(bf16)
            acc = acc + lax.dot_general(
                member,
                jnp.concatenate([hi, lo], 0),
                (((1,), (1,)), ((), ())),
                preferred_element_type=f32,
            )
    pooled = (acc[:, :group] + acc[:, group:]) / row_len
    pooled = jnp.concatenate([pooled, jnp.zeros((segs, LANES - group), f32)], 1)
    shift = lax.rem(lax.axis_index("seq"), LANES // group) * group
    pooled = pltpu.roll(pooled, shift, 1)
    out[:, subs * group :, :] = pooled.reshape(seq_count, owned, LANES)


def back_kernel(taken, mixed, pooled, *, seq_count, group, subs):
    channels = seq_count * group
    for sub in range(subs):
        block = taken[:, sub * group : (sub + 1) * group, :].reshape(channels, LANES)
        mixed[sub * LANES : (sub + 1) * LANES, :] = block.T
    per_lane = LANES // group
    for half in range(channels // LANES):
        total = taken[half * per_lane, subs * group :, :]
        for at in range(half * per_lane + 1, (half + 1) * per_lane):
            total = total + taken[at, subs * group :, :]
        pooled[:, half * LANES : (half + 1) * LANES] = total


def on_device(signal, filter_taps, out_gate, skip_gain, lengths, row_of_segment):
    seq_count = lax.axis_size("seq")
    block_rows, channels = signal.shape
    group = channels // seq_count
    subs = block_rows // LANES
    segs = lengths.shape[0]
    owned = segs // seq_count
    sizes = dict(seq_count=seq_count, group=group, subs=subs)
    sent = pl.pallas_call(
        functools.partial(turn_kernel, **sizes),
        out_shape=pltpu.VMEM((seq_count, 3 * subs * group, LANES), f32),
        interpret=INTERPRET,
        name="turn",
    )(signal, filter_taps, out_gate, skip_gain.reshape(1, channels))
    taken = lax.all_to_all(sent, "seq", 0, 0)
    taken = taken.reshape(seq_count * 3 * subs * group, LANES)
    taken = pltpu.with_memory_space_constraint(taken, pltpu.VMEM)
    consts = [jnp.asarray(table) for table in tables(seq_count, subs)]
    mixed_sent = pl.pallas_call(
        functools.partial(conv_kernel, **sizes),
        out_shape=pltpu.VMEM((seq_count, subs * group + owned, LANES), f32),
        scratch_shapes=[pltpu.VMEM((seq_count * subs * group, LANES), f32)],
        interpret=INTERPRET,
        name="conv",
    )(
        taken,
        lengths.reshape(1, segs),
        row_of_segment.reshape(1, segs),
        *consts,
    )
    back = lax.all_to_all(mixed_sent, "seq", 0, 0)
    back = pltpu.with_memory_space_constraint(back, pltpu.VMEM)
    return pl.pallas_call(
        functools.partial(back_kernel, **sizes),
        out_shape=(
            jax.ShapeDtypeStruct((block_rows, channels), f32),
            jax.ShapeDtypeStruct((owned, channels), f32),
        ),
        interpret=INTERPRET,
        name="back",
    )(back)


def solution(mesh):
    placed = (P("seq", "chan"), P("seq", "chan"), P("seq", "chan"), P("chan"), P(), P())
    return jax.shard_map(
        on_device,
        mesh=mesh,
        in_specs=placed,
        out_specs=(P("seq", "chan"), P("seq", "chan")),
        check_vma=False,
    )
```

```python
import functools
import math

import jax
import jax.numpy as jnp
import numpy as np
from jax import lax
from jax.experimental import pallas as pl
from jax.experimental.pallas import tpu as pltpu
from jax.sharding import PartitionSpec as P


LANES = 128
FWD = 4
INV = 4
INTERPRET = False
bf16 = jnp.bfloat16
f32 = jnp.float32


def split_const(value):
    hi = value.astype(bf16)
    return hi, (value - hi.astype(np.float64)).astype(bf16)


@functools.lru_cache(None)
def tables(seq_count, subs):
    rows = seq_count * subs
    total = rows * LANES
    t1 = np.array([device * subs + sub for sub in range(subs) for device in range(seq_count)], np.float64)
    k1 = np.arange(rows, dtype=np.float64)
    t2 = np.arange(LANES, dtype=np.float64)
    first = -2.0 * math.pi * (k1[:, None] + 0.25) * t1[None, :] / rows
    first = np.concatenate([np.cos(first), np.sin(first)], 0)
    hi, lo = split_const(first)
    first3 = np.concatenate([hi, lo, hi], 1)
    twist = -2.0 * math.pi * (k1[:, None] + 0.25) * t2[None, :] / total
    twist = np.stack([np.cos(twist), np.sin(twist)]).astype(np.float32)
    angle = 2.0 * math.pi * (np.outer(t2, t2) % LANES) / LANES
    cos, sin = np.cos(angle), np.sin(angle)
    forward = np.block([[cos, -sin], [sin, cos]])
    hi, lo = split_const(forward)
    forward3 = np.concatenate([hi, hi, lo], 0)
    hi, lo = split_const(forward.T / total)
    inverse3 = np.concatenate([hi, hi, lo], 0)
    last = 2.0 * math.pi * t1[:, None] * (k1[None, :] + 0.25) / rows
    hi, lo = split_const(np.concatenate([np.cos(last), -np.sin(last)], 1))
    last3 = np.concatenate([hi, lo, hi], 1)
    return first3, twist, forward3, inverse3, last3


def split(value):
    hi = value.astype(bf16)
    lo = (value - hi.astype(f32)).astype(bf16)
    return hi, lo


def mm(left, right):
    return lax.dot_general(left, right, (((1,), (0,)), ((), ())), preferred_element_type=f32)


def turn_kernel(signal, taps, gate, skip, out, *, seq_count, group, subs):
    at_start = lax.axis_index("seq") == 0
    for sub in range(subs):
        rows = slice(sub * LANES, (sub + 1) * LANES)
        for which, ref in enumerate((signal, taps, gate)):
            value = ref[rows, :]
            if which == 1 and sub == 0:
                place = lax.broadcasted_iota(jnp.int32, value.shape, 0)
                value = value + jnp.where((place == 0) & at_start, skip[...], 0.0)
            base = (sub * 3 + which) * group
            out[:, base : base + group, :] = value.T.reshape(seq_count, group, LANES)


def conv_kernel(
    taken, lengths, row_of, first3, twist, forward3, inverse3, last3, out, conv, turned, product, *, seq_count, group, subs
):
    rows = seq_count * subs
    per = 3 * subs * group
    twist_re, twist_im = twist[0], twist[1]

    def gather(which, channel):
        parts = []
        for sub in range(subs):
            start = (sub * 3 + which) * group + channel
            parts.append(taken[pl.ds(start, seq_count, stride=per), :])
        return jnp.concatenate(parts, 0)

    for channel in range(group):
        both = jnp.concatenate([gather(0, channel), gather(1, channel)], 1)
        hi, lo = split(both)
        stage = mm(first3[...], jnp.concatenate([hi, hi, lo], 0))
        for side in range(2):
            lanes = slice(side * LANES, (side + 1) * LANES)
            re, im = stage[:rows, lanes], stage[rows:, lanes]
            at = slice((2 * channel + side) * rows, (2 * channel + side + 1) * rows)
            for half, value in enumerate((re * twist_re - im * twist_im, re * twist_im + im * twist_re)):
                lanes_out = slice(half * LANES, (half + 1) * LANES)
                hi, lo = split(value)
                turned[at, lanes_out] = hi
                turned[at, 2 * LANES + half * LANES : 2 * LANES + (half + 1) * LANES] = lo

    def three(ref, at, table):
        hi, lo = ref[at, : 2 * LANES], ref[at, 2 * LANES :]
        high = table[: 2 * LANES, :]
        return mm(hi, high) + mm(lo, high) + mm(hi, table[4 * LANES :, :])

    for block in range(group // FWD):
        spec = three(turned, slice(block * FWD * 2 * rows, (block + 1) * FWD * 2 * rows), forward3)
        for at in range(FWD):
            channel = block * FWD + at
            left = spec[(2 * at) * rows : (2 * at + 1) * rows]
            right = spec[(2 * at + 1) * rows : (2 * at + 2) * rows]
            left_re, left_im = left[:, :LANES], left[:, LANES:]
            right_re, right_im = right[:, :LANES], right[:, LANES:]
            products = (left_re * right_re - left_im * right_im, left_re * right_im + left_im * right_re)
            here = slice(channel * rows, (channel + 1) * rows)
            for half, value in enumerate(products):
                hi, lo = split(value)
                product[here, half * LANES : (half + 1) * LANES] = hi
                product[here, (2 + half) * LANES : (3 + half) * LANES] = lo

    for block in range(group // INV):
        back = three(product, slice(block * INV * rows, (block + 1) * INV * rows), inverse3)
        for pair in range(INV // 2):
            values = []
            for at in (2 * pair, 2 * pair + 1):
                re, im = back[at * rows : (at + 1) * rows, :LANES], back[at * rows : (at + 1) * rows, LANES:]
                values.append(
                    jnp.concatenate([re * twist_re + im * twist_im, im * twist_re - re * twist_im], 0)
                )
            hi, lo = split(jnp.concatenate(values, 1))
            result = mm(last3[...], jnp.concatenate([hi, hi, lo], 0))
            for at in range(2):
                channel = block * INV + pair * 2 + at
                for sub in range(subs):
                    conv[pl.ds(sub * group + channel, seq_count, stride=subs * group), :] = result[
                        sub * seq_count : (sub + 1) * seq_count, at * LANES : (at + 1) * LANES
                    ]

    segs = lengths.shape[1]
    owned = segs // seq_count
    seg_len = lengths[...].astype(f32)
    seg_at = lax.broadcasted_iota(jnp.int32, (segs, segs), 1)
    hit = row_of[...] == lax.broadcasted_iota(jnp.int32, (segs, segs), 0)
    which_seg = jnp.sum(jnp.where(hit, seg_at, 0).astype(f32), axis=1, keepdims=True)
    row_len = jnp.sum(jnp.where(hit, seg_len, 0.0), axis=1, keepdims=True)
    row_start = jnp.sum(jnp.where(seg_at.astype(f32) < which_seg, seg_len, 0.0), axis=1, keepdims=True)
    token = lax.broadcasted_iota(jnp.int32, (segs, 2 * LANES), 1)
    past_start = token - row_start.astype(jnp.int32)
    to_end = (row_len.astype(jnp.int32) - 1 - past_start).astype(jnp.int16)
    past_start = past_start.astype(jnp.int16)
    one, zero = jnp.ones((segs, 2 * LANES), bf16), jnp.zeros((segs, 2 * LANES), bf16)
    acc = jnp.zeros((segs, 2 * group), f32)
    for device in range(seq_count):
        for step in range(subs // 2):
            halves = []
            for sub in (2 * step, 2 * step + 1):
                base = (device * subs + sub) * group
                from_row = device * per + (sub * 3 + 2) * group
                mixed = conv[base : base + group, :] * taken[from_row : from_row + group, :]
                out[device, sub * group : (sub + 1) * group, :] = mixed
                halves.append(mixed)
            hi, lo = split(jnp.concatenate(halves, 1))
            offset = (device * subs + 2 * step) * LANES
            member = jnp.where(
                (past_start >= jnp.int16(-offset)) & (to_end >= jnp.int16(offset)), one, zero
            )
            acc = acc + lax.dot_general(
                member,
                jnp.concatenate([hi, lo], 0),
                (((1,), (1,)), ((), ())),
                preferred_element_type=f32,
            )
    pooled = (acc[:, :group] + acc[:, group:]) / row_len
    pooled = jnp.concatenate([pooled, jnp.zeros((segs, LANES - group), f32)], 1)
    shift = lax.rem(lax.axis_index("seq"), LANES // group) * group
    pooled = pltpu.roll(pooled, shift, 1)
    out[:, subs * group :, :] = pooled.reshape(seq_count, owned, LANES)


def back_kernel(taken, mixed, pooled, *, seq_count, group, subs):
    channels = seq_count * group
    for sub in range(subs):
        block = taken[:, sub * group : (sub + 1) * group, :].reshape(channels, LANES)
        mixed[sub * LANES : (sub + 1) * LANES, :] = block.T
    per_lane = LANES // group
    for half in range(channels // LANES):
        total = taken[half * per_lane, subs * group :, :]
        for at in range(half * per_lane + 1, (half + 1) * per_lane):
            total = total + taken[at, subs * group :, :]
        pooled[:, half * LANES : (half + 1) * LANES] = total


def on_device(signal, filter_taps, out_gate, skip_gain, lengths, row_of_segment):
    seq_count = lax.axis_size("seq")
    block_rows, channels = signal.shape
    group = channels // seq_count
    subs = block_rows // LANES
    segs = lengths.shape[0]
    owned = segs // seq_count
    sizes = dict(seq_count=seq_count, group=group, subs=subs)
    sent = pl.pallas_call(
        functools.partial(turn_kernel, **sizes),
        out_shape=pltpu.VMEM((seq_count, 3 * subs * group, LANES), f32),
        interpret=INTERPRET,
        name="turn",
    )(signal, filter_taps, out_gate, skip_gain.reshape(1, channels))
    taken = lax.all_to_all(sent, "seq", 0, 0)
    taken = taken.reshape(seq_count * 3 * subs * group, LANES)
    taken = pltpu.with_memory_space_constraint(taken, pltpu.VMEM)
    consts = [jnp.asarray(table) for table in tables(seq_count, subs)]
    mixed_sent = pl.pallas_call(
        functools.partial(conv_kernel, **sizes),
        out_shape=pltpu.VMEM((seq_count, subs * group + owned, LANES), f32),
        scratch_shapes=[
            pltpu.VMEM((seq_count * subs * group, LANES), f32),
            pltpu.VMEM((2 * group * seq_count * subs, 4 * LANES), bf16),
            pltpu.VMEM((group * seq_count * subs, 4 * LANES), bf16),
        ],
        interpret=INTERPRET,
        name="conv",
    )(
        taken,
        lengths.reshape(1, segs),
        row_of_segment.reshape(1, segs),
        *consts,
    )
    back = lax.all_to_all(mixed_sent, "seq", 0, 0)
    back = pltpu.with_memory_space_constraint(back, pltpu.VMEM)
    return pl.pallas_call(
        functools.partial(back_kernel, **sizes),
        out_shape=(
            jax.ShapeDtypeStruct((block_rows, channels), f32),
            jax.ShapeDtypeStruct((owned, channels), f32),
        ),
        interpret=INTERPRET,
        name="back",
    )(back)


def solution(mesh):
    placed = (P("seq", "chan"), P("seq", "chan"), P("seq", "chan"), P("chan"), P(), P())
    return jax.shard_map(
        on_device,
        mesh=mesh,
        in_specs=placed,
        out_specs=(P("seq", "chan"), P("seq", "chan")),
        check_vma=False,
    )
```

```python
import functools
import math

import jax
import jax.numpy as jnp
import numpy as np
from jax import lax
from jax.experimental import pallas as pl
from jax.experimental.pallas import tpu as pltpu
from jax.sharding import PartitionSpec as P


LANES = 128
VMEM_LIMIT = 24 << 20
FWD = 8
ACC = 2
INV = 4
INTERPRET = False
bf16 = jnp.bfloat16
f32 = jnp.float32


def split_const(value):
    hi = value.astype(bf16)
    return hi, (value - hi.astype(np.float64)).astype(bf16)


@functools.lru_cache(None)
def tables(seq_count, subs):
    rows = seq_count * subs
    total = rows * LANES
    t1 = np.array([device * subs + sub for sub in range(subs) for device in range(seq_count)], np.float64)
    k1 = np.arange(rows, dtype=np.float64)
    t2 = np.arange(LANES, dtype=np.float64)
    first = -2.0 * math.pi * (k1[:, None] + 0.25) * t1[None, :] / rows
    hi, lo = split_const(np.concatenate([np.cos(first), np.sin(first)], 0))
    first3 = np.concatenate([hi, lo, hi, np.zeros_like(hi)], 1)
    angle = 2.0 * math.pi * (np.outer(t2, t2) % LANES) / LANES
    cos, sin = np.cos(angle), np.sin(angle)
    forward = np.block([[cos, -sin], [sin, cos]])
    last = 2.0 * math.pi * t1[:, None] * (k1[None, :] + 0.25) / rows
    last_hi, last_lo = split_const(np.concatenate([np.cos(last), -np.sin(last)], 1))
    twist = -2.0 * math.pi * (k1[:, None] + 0.25) * t2[None, :] / total
    twist = np.concatenate([np.cos(twist), np.sin(twist)], 1)
    high, middle = split_const(twist)
    low = (twist - high.astype(np.float64) - middle.astype(np.float64)).astype(bf16)
    parts = [
        *split_const(forward),
        *split_const(forward.T / total),
        first3,
        np.concatenate([last_hi, last_lo], 1),
        np.concatenate([last_hi, np.zeros_like(last_hi)], 1),
        high,
        middle,
        low,
    ]
    return np.concatenate(parts, 0)


def split(value):
    hi = value.astype(bf16)
    lo = (value - hi.astype(f32)).astype(bf16)
    return hi, lo


def mm(left, right):
    return lax.dot_general(left, right, (((1,), (0,)), ((), ())), preferred_element_type=f32)


def turn_kernel(
    signal, taps, gate, skip, lengths, row_of, consts, out, bounds, sizes, table,
    big, row, ints, sems, small_sems,
    *, seq_count, group, subs
):
    small = (
        pltpu.make_async_copy(lengths, ints.at[0], small_sems.at[0]),
        pltpu.make_async_copy(row_of, ints.at[1], small_sems.at[1]),
        pltpu.make_async_copy(skip, row, small_sems.at[2]),
    )
    for copy in small:
        copy.start()
    constant = pltpu.make_async_copy(consts, table, small_sems.at[3])
    large = []
    for which, ref in enumerate((signal, taps, gate)):
        for sub in range(subs):
            rows = pl.ds(sub * LANES, LANES)
            at = which * subs + sub
            large.append(pltpu.make_async_copy(ref.at[rows, :], big.at[at], sems.at[at]))
            large[-1].start()
    constant.start()
    for copy in small:
        copy.wait()

    segs = ints.shape[2]
    seg_len = jnp.broadcast_to(ints[0].astype(f32), (segs, segs)).T
    seg_row = jnp.broadcast_to(ints[1].astype(f32), (segs, segs)).T
    seg_at = lax.broadcasted_iota(jnp.int32, (segs, segs), 0).astype(f32)
    hit = seg_row == lax.broadcasted_iota(jnp.int32, (segs, segs), 1).astype(f32)
    which_seg = jnp.sum(jnp.where(hit, seg_at, 0.0), axis=0, keepdims=True)
    row_len = jnp.sum(jnp.where(hit, seg_len, 0.0), axis=0, keepdims=True)
    row_start = jnp.sum(jnp.where(seg_at < which_seg, seg_len, 0.0), axis=0, keepdims=True)
    bounds[...] = jnp.broadcast_to(row_start, bounds.shape)
    sizes[...] = jnp.broadcast_to(row_len, sizes.shape)

    at_start = lax.axis_index("seq") == 0
    for which in range(3):
        for sub in range(subs):
            large[which * subs + sub].wait()
        for sub in range(subs):
            value = big[which * subs + sub]
            if which == 1 and sub == 0:
                place = lax.broadcasted_iota(jnp.int32, value.shape, 0)
                value = value + jnp.where((place == 0) & at_start, row[...], 0.0)
            base = (sub * 3 + which) * group
            out[:, base : base + group, :] = value.T.reshape(seq_count, group, LANES)
    constant.wait()


def conv_kernel(
    taken, bounds, sizes, table, out, conv, turned, product, unturned, spread, *, seq_count, group, subs
):
    rows = seq_count * subs
    per = 3 * subs * group
    wide = 2 * LANES

    def tabled(at, count, lanes=wide):
        return table[at : at + count, :lanes]

    at = 4 * wide
    first3 = tabled(at, 2 * rows, 3 * rows)
    at += 2 * rows
    last3 = jnp.concatenate([tabled(at, rows), tabled(at + rows, rows, LANES)], 1)
    at += 2 * rows
    twist = tabled(at, rows).astype(f32) + tabled(at + rows, rows).astype(f32)
    twist = twist + tabled(at + 2 * rows, rows).astype(f32)
    twist_re, twist_im = twist[:, :LANES], twist[:, LANES:]

    pitch = 2 * subs * group + 1
    for device in range(seq_count):
        for sub in range(subs):
            for which in range(2):
                base = device * pitch + (sub * 2 + which) * group
                from_row = device * per + (sub * 3 + which) * group
                spread[base : base + group, :] = taken[from_row : from_row + group, :]

    def gather(which, channel):
        parts = []
        for sub in range(subs):
            start = (sub * 2 + which) * group + channel
            parts.append(spread[pl.ds(start, seq_count, stride=pitch), :])
        return jnp.concatenate(parts, 0)

    for channel in range(group):
        both = jnp.concatenate([gather(0, channel), gather(1, channel)], 1)
        hi, lo = split(both)
        stage = mm(first3, jnp.concatenate([hi, hi, lo], 0))
        for side in range(2):
            lanes = slice(side * LANES, (side + 1) * LANES)
            re, im = stage[:rows, lanes], stage[rows:, lanes]
            at = slice((2 * channel + side) * rows, (2 * channel + side + 1) * rows)
            for half, value in enumerate((re * twist_re - im * twist_im, re * twist_im + im * twist_re)):
                lanes_out = slice(half * LANES, (half + 1) * LANES)
                hi, lo = split(value)
                turned[at, lanes_out] = hi
                turned[at, 2 * LANES + half * LANES : 2 * LANES + (half + 1) * LANES] = lo

    def three(ref, at, base):
        high, low = tabled(base, wide), tabled(base + wide, wide)
        return mm(jnp.concatenate([ref[at, :], ref[at, :wide]], 1), jnp.concatenate([high, high, low], 0))

    for block in range(group // FWD):
        spec = three(turned, slice(block * FWD * 2 * rows, (block + 1) * FWD * 2 * rows), 0)
        for at in range(FWD):
            channel = block * FWD + at
            left = spec[(2 * at) * rows : (2 * at + 1) * rows]
            right = spec[(2 * at + 1) * rows : (2 * at + 2) * rows]
            left_re, left_im = left[:, :LANES], left[:, LANES:]
            right_re, right_im = right[:, :LANES], right[:, LANES:]
            products = (left_re * right_re - left_im * right_im, left_re * right_im + left_im * right_re)
            here = slice(channel * rows, (channel + 1) * rows)
            for half, value in enumerate(products):
                hi, lo = split(value)
                product[here, half * LANES : (half + 1) * LANES] = hi
                product[here, (2 + half) * LANES : (3 + half) * LANES] = lo

    for block in range(group // INV):
        back = three(product, slice(block * INV * rows, (block + 1) * INV * rows), 2 * wide)
        for at in range(INV):
            channel = block * INV + at
            lanes = slice(channel % 2 * LANES, (channel % 2 + 1) * LANES)
            re, im = back[at * rows : (at + 1) * rows, :LANES], back[at * rows : (at + 1) * rows, LANES:]
            values = (re * twist_re + im * twist_im, im * twist_re - re * twist_im)
            for half, value in enumerate(values):
                hi, lo = split(value)
                base = channel // 2 * 4 * rows + half * rows
                unturned[base : base + rows, lanes] = hi
                unturned[base + 2 * rows : base + 3 * rows, lanes] = lo

    for pair in range(group // 2):
        hi = unturned[pair * 4 * rows : pair * 4 * rows + 2 * rows, :]
        lo = unturned[pair * 4 * rows + 2 * rows : (pair + 1) * 4 * rows, :]
        result = mm(last3, jnp.concatenate([hi, hi, lo], 0))
        for at in range(2):
            for sub in range(subs):
                start = sub * group + pair * 2 + at
                conv[pl.ds(start, seq_count, stride=subs * group + 1), :] = result[
                    sub * seq_count : (sub + 1) * seq_count, at * LANES : (at + 1) * LANES
                ]

    segs = sizes.shape[1]
    owned = segs // seq_count
    past_start = lax.broadcasted_iota(jnp.int32, (wide, segs), 0) - bounds[:1, :].astype(jnp.int32)
    to_end = (sizes[:1, :].astype(jnp.int32) - 1 - past_start).astype(jnp.int16)
    past_start = past_start.astype(jnp.int16)
    one, zero = jnp.ones((wide, segs), bf16), jnp.zeros((wide, segs), bf16)
    sums = [jnp.zeros((2 * group, segs), f32) for _ in range(ACC)]
    for device in range(seq_count):
        for step in range(subs // 2):
            halves = []
            for sub in (2 * step, 2 * step + 1):
                base = device * (subs * group + 1) + sub * group
                from_row = device * per + (sub * 3 + 2) * group
                mixed = conv[base : base + group, :] * taken[from_row : from_row + group, :]
                out[device, sub * group : (sub + 1) * group, :] = mixed
                halves.append(mixed)
            hi, lo = split(jnp.concatenate(halves, 1))
            offset = (device * subs + 2 * step) * LANES
            member = jnp.where(
                (past_start >= jnp.int16(-offset)) & (to_end >= jnp.int16(offset)), one, zero
            )
            which = (device * (subs // 2) + step) % ACC
            sums[which] = sums[which] + mm(jnp.concatenate([hi, lo], 0), member)
    acc = sum(sums[1:], sums[0])
    pooled = (acc[:group] + acc[group:]) / sizes[:group, :]
    pooled = jnp.concatenate([pooled, jnp.zeros((LANES - group, segs), f32)], 0).T
    shift = lax.rem(lax.axis_index("seq"), LANES // group) * group
    pooled = pltpu.roll(pooled, shift, 1)
    out[:, subs * group :, :] = pooled.reshape(seq_count, owned, LANES)


def back_kernel(taken, mixed, pooled, *, seq_count, group, subs):
    channels = seq_count * group
    for sub in range(subs):
        block = taken[:, sub * group : (sub + 1) * group, :].reshape(channels, LANES)
        mixed[sub * LANES : (sub + 1) * LANES, :] = block.T
    per_lane = LANES // group
    for half in range(channels // LANES):
        total = taken[half * per_lane, subs * group :, :]
        for at in range(half * per_lane + 1, (half + 1) * per_lane):
            total = total + taken[at, subs * group :, :]
        pooled[:, half * LANES : (half + 1) * LANES] = total


def in_vmem(value):
    return pltpu.with_memory_space_constraint(value, pltpu.VMEM)


def on_device(signal, filter_taps, out_gate, skip_gain, lengths, row_of_segment):
    seq_count = lax.axis_size("seq")
    block_rows, channels = signal.shape
    group = channels // seq_count
    subs = block_rows // LANES
    segs = lengths.shape[0]
    owned = segs // seq_count
    sizes = dict(seq_count=seq_count, group=group, subs=subs)
    anywhere = pl.BlockSpec(memory_space=pltpu.HBM)
    consts = jnp.asarray(tables(seq_count, subs))
    sent, bounds, row_sizes, table = pl.pallas_call(
        functools.partial(turn_kernel, **sizes),
        in_specs=[anywhere] * 7,
        out_shape=(
            pltpu.VMEM((seq_count, 3 * subs * group, LANES), f32),
            pltpu.VMEM((2 * group, segs), f32),
            pltpu.VMEM((2 * group, segs), f32),
            pltpu.VMEM(consts.shape, bf16),
        ),
        scratch_shapes=[
            pltpu.VMEM((3 * subs, LANES, channels), f32),
            pltpu.VMEM((1, channels), f32),
            pltpu.VMEM((2, 1, segs), jnp.int32),
            pltpu.SemaphoreType.DMA((3 * subs,)),
            pltpu.SemaphoreType.DMA((4,)),
        ],
        interpret=INTERPRET,
        name="turn",
        compiler_params=pltpu.CompilerParams(vmem_limit_bytes=VMEM_LIMIT),
    )(
        *(
            pltpu.with_memory_space_constraint(value, pltpu.HBM)
            for value in (
                signal,
                filter_taps,
                out_gate,
                skip_gain.reshape(1, channels),
                lengths.reshape(1, segs),
                row_of_segment.reshape(1, segs),
                consts,
            )
        )
    )
    taken = lax.all_to_all(sent, "seq", 0, 0)
    taken = in_vmem(taken.reshape(seq_count * 3 * subs * group, LANES))
    mixed_sent = pl.pallas_call(
        functools.partial(conv_kernel, **sizes),
        out_shape=pltpu.VMEM((seq_count, subs * group + owned, LANES), f32),
        scratch_shapes=[
            pltpu.VMEM((seq_count * (subs * group + 1), LANES), f32),
            pltpu.VMEM((2 * group * seq_count * subs, 4 * LANES), bf16),
            pltpu.VMEM((group * seq_count * subs, 4 * LANES), bf16),
            pltpu.VMEM((2 * group * seq_count * subs, 2 * LANES), bf16),
            pltpu.VMEM((seq_count * (2 * subs * group + 1), LANES), f32),
        ],
        interpret=INTERPRET,
        name="conv",
        compiler_params=pltpu.CompilerParams(vmem_limit_bytes=VMEM_LIMIT),
    )(taken, in_vmem(bounds), in_vmem(row_sizes), in_vmem(table))
    back = lax.all_to_all(mixed_sent, "seq", 0, 0)
    back = in_vmem(back)
    return pl.pallas_call(
        functools.partial(back_kernel, **sizes),
        out_shape=(
            jax.ShapeDtypeStruct((block_rows, channels), f32),
            jax.ShapeDtypeStruct((owned, channels), f32),
        ),
        interpret=INTERPRET,
        name="back",
        compiler_params=pltpu.CompilerParams(vmem_limit_bytes=VMEM_LIMIT),
    )(back)


def solution(mesh):
    placed = (P("seq", "chan"), P("seq", "chan"), P("seq", "chan"), P("chan"), P(), P())
    return jax.shard_map(
        on_device,
        mesh=mesh,
        in_specs=placed,
        out_specs=(P("seq", "chan"), P("seq", "chan")),
        check_vma=False,
    )
```

```python
import functools
import math

import jax
import jax.numpy as jnp
import numpy as np
from jax import lax
from jax.experimental import pallas as pl
from jax.experimental.pallas import tpu as pltpu
from jax.sharding import PartitionSpec as P


LANES = 128
VMEM_LIMIT = 24 << 20
FWD = 8
ACC = 2
INV = 4
INTERPRET = False
OUT_ORDER = [10, 6, 12, 2, 13, 4, 5, 7, 3, 0, 9, 14, 15, 8, 1, 11]
BACK_ORDER = OUT_ORDER
bf16 = jnp.bfloat16
f32 = jnp.float32


def order_of(wanted, seq_count):
    return wanted if len(wanted) == seq_count else list(range(seq_count))


def exchange(value, order):
    return lax.all_to_all(value, "seq", 0, 0, axis_index_groups=[order])


def place_in(order):
    mine = lax.axis_index("seq")
    place = jnp.int32(0)
    for at, device in enumerate(order):
        place = jnp.where(mine == device, at, place)
    return place


def split_const(value):
    hi = value.astype(bf16)
    return hi, (value - hi.astype(np.float64)).astype(bf16)


@functools.lru_cache(None)
def tables(seq_count, subs):
    rows = seq_count * subs
    total = rows * LANES
    order = order_of(OUT_ORDER, seq_count)
    t1 = np.array([device * subs + sub for sub in range(subs) for device in order], np.float64)
    k1 = np.arange(rows, dtype=np.float64)
    t2 = np.arange(LANES, dtype=np.float64)
    first = -2.0 * math.pi * (k1[:, None] + 0.25) * t1[None, :] / rows
    hi, lo = split_const(np.concatenate([np.cos(first), np.sin(first)], 0))
    first3 = np.concatenate([hi, lo, hi, np.zeros_like(hi)], 1)
    angle = 2.0 * math.pi * (np.outer(t2, t2) % LANES) / LANES
    cos, sin = np.cos(angle), np.sin(angle)
    forward = np.block([[cos, -sin], [sin, cos]])
    last = 2.0 * math.pi * t1[:, None] * (k1[None, :] + 0.25) / rows
    last_hi, last_lo = split_const(np.concatenate([np.cos(last), np.sin(last)], 1) / total)
    twist = -2.0 * math.pi * (k1[:, None] + 0.25) * t2[None, :] / total
    twist = np.concatenate([np.cos(twist), np.sin(twist)], 1)
    high, middle = split_const(twist)
    low = (twist - high.astype(np.float64) - middle.astype(np.float64)).astype(bf16)
    parts = [
        *split_const(forward),
        first3,
        np.concatenate([last_hi, last_lo], 1),
        np.concatenate([last_hi, np.zeros_like(last_hi)], 1),
        high,
        middle,
        low,
    ]
    return np.concatenate(parts, 0)


def split(value):
    hi = value.astype(bf16)
    lo = (value - hi.astype(f32)).astype(bf16)
    return hi, lo


def mm(left, right):
    return lax.dot_general(left, right, (((1,), (0,)), ((), ())), preferred_element_type=f32)


def turn_kernel(
    signal, taps, gate, skip, lengths, row_of, consts, out, bounds, sizes, table,
    big, row, ints, sems, small_sems,
    *, seq_count, group, subs
):
    small = (
        pltpu.make_async_copy(lengths, ints.at[0], small_sems.at[0]),
        pltpu.make_async_copy(row_of, ints.at[1], small_sems.at[1]),
        pltpu.make_async_copy(skip, row, small_sems.at[2]),
    )
    for copy in small:
        copy.start()
    constant = pltpu.make_async_copy(consts, table, small_sems.at[3])
    large = []
    for which, ref in enumerate((signal, taps, gate)):
        large.append(pltpu.make_async_copy(ref, big.at[which], sems.at[which]))
        large[-1].start()
    constant.start()
    for copy in small:
        copy.wait()

    segs = ints.shape[2]
    seg_len = jnp.broadcast_to(ints[0].astype(f32), (segs, segs)).T
    seg_row = jnp.broadcast_to(ints[1].astype(f32), (segs, segs)).T
    seg_at = lax.broadcasted_iota(jnp.int32, (segs, segs), 0).astype(f32)
    hit = seg_row == lax.broadcasted_iota(jnp.int32, (segs, segs), 1).astype(f32)
    which_seg = jnp.sum(jnp.where(hit, seg_at, 0.0), axis=0, keepdims=True)
    row_len = jnp.sum(jnp.where(hit, seg_len, 0.0), axis=0, keepdims=True)
    row_start = jnp.sum(jnp.where(seg_at < which_seg, seg_len, 0.0), axis=0, keepdims=True)
    bounds[...] = jnp.broadcast_to(row_start, bounds.shape)
    sizes[...] = jnp.broadcast_to(row_len, sizes.shape)

    at_start = lax.axis_index("seq") == 0
    for which in range(3):
        large[which].wait()
        for sub in range(subs):
            value = big[which, sub * LANES : (sub + 1) * LANES, :]
            if which == 1 and sub == 0:
                place = lax.broadcasted_iota(jnp.int32, value.shape, 0)
                value = value + jnp.where((place == 0) & at_start, row[...], 0.0)
            base = (sub * 3 + which) * group
            out[:, base : base + group, :] = value.T.reshape(seq_count, group, LANES)
    constant.wait()


def conv_kernel(
    taken, bounds, sizes, table, out, conv, turned, product, unturned, spread, *, seq_count, group, subs
):
    rows = seq_count * subs
    per = 3 * subs * group
    wide = 2 * LANES

    def tabled(at, count, lanes=wide):
        return table[at : at + count, :lanes]

    at = 2 * wide
    first3 = tabled(at, 2 * rows, 3 * rows)
    at += 2 * rows
    last3 = jnp.concatenate([tabled(at, rows), tabled(at + rows, rows, LANES)], 1)
    at += 2 * rows
    twist = tabled(at, rows).astype(f32) + tabled(at + rows, rows).astype(f32)
    twist = twist + tabled(at + 2 * rows, rows).astype(f32)
    twist_re, twist_im = twist[:, :LANES], twist[:, LANES:]

    pitch = 2 * subs * group + 1
    for device in range(seq_count):
        for sub in range(subs):
            for which in range(2):
                base = device * pitch + (sub * 2 + which) * group
                from_row = device * per + (sub * 3 + which) * group
                spread[base : base + group, :] = taken[from_row : from_row + group, :]

    def gather(which, channel):
        parts = []
        for sub in range(subs):
            start = (sub * 2 + which) * group + channel
            parts.append(spread[pl.ds(start, seq_count, stride=pitch), :])
        return jnp.concatenate(parts, 0)

    for channel in range(group):
        both = jnp.concatenate([gather(0, channel), gather(1, channel)], 1)
        hi, lo = split(both)
        stage = mm(first3, jnp.concatenate([hi, hi, lo], 0))
        for side in range(2):
            lanes = slice(side * LANES, (side + 1) * LANES)
            re, im = stage[:rows, lanes], stage[rows:, lanes]
            at = slice((2 * channel + side) * rows, (2 * channel + side + 1) * rows)
            for half, value in enumerate((re * twist_re - im * twist_im, re * twist_im + im * twist_re)):
                lanes_out = slice(half * LANES, (half + 1) * LANES)
                hi, lo = split(value)
                turned[at, lanes_out] = hi
                turned[at, 2 * LANES + half * LANES : 2 * LANES + (half + 1) * LANES] = lo

    def three(ref, at):
        high, low = tabled(0, wide), tabled(wide, wide)
        return mm(jnp.concatenate([ref[at, :], ref[at, :wide]], 1), jnp.concatenate([high, high, low], 0))

    for block in range(group // FWD):
        spec = three(turned, slice(block * FWD * 2 * rows, (block + 1) * FWD * 2 * rows))
        for at in range(FWD):
            channel = block * FWD + at
            left = spec[(2 * at) * rows : (2 * at + 1) * rows]
            right = spec[(2 * at + 1) * rows : (2 * at + 2) * rows]
            left_re, left_im = left[:, :LANES], left[:, LANES:]
            right_re, right_im = right[:, :LANES], right[:, LANES:]
            products = (left_re * right_re - left_im * right_im, -(left_re * right_im) - left_im * right_re)
            here = slice(channel * rows, (channel + 1) * rows)
            for half, value in enumerate(products):
                hi, lo = split(value)
                product[here, half * LANES : (half + 1) * LANES] = hi
                product[here, (2 + half) * LANES : (3 + half) * LANES] = lo

    for block in range(group // INV):
        back = three(product, slice(block * INV * rows, (block + 1) * INV * rows))
        for at in range(INV):
            channel = block * INV + at
            lanes = slice(channel % 2 * LANES, (channel % 2 + 1) * LANES)
            re, im = back[at * rows : (at + 1) * rows, :LANES], back[at * rows : (at + 1) * rows, LANES:]
            values = (re * twist_re - im * twist_im, im * twist_re + re * twist_im)
            for half, value in enumerate(values):
                hi, lo = split(value)
                base = channel // 2 * 4 * rows + half * rows
                unturned[base : base + rows, lanes] = hi
                unturned[base + 2 * rows : base + 3 * rows, lanes] = lo

    for pair in range(group // 2):
        hi = unturned[pair * 4 * rows : pair * 4 * rows + 2 * rows, :]
        lo = unturned[pair * 4 * rows + 2 * rows : (pair + 1) * 4 * rows, :]
        result = mm(last3, jnp.concatenate([hi, hi, lo], 0))
        for at in range(2):
            for sub in range(subs):
                start = sub * group + pair * 2 + at
                conv[pl.ds(start, seq_count, stride=subs * group + 1), :] = result[
                    sub * seq_count : (sub + 1) * seq_count, at * LANES : (at + 1) * LANES
                ]

    segs = sizes.shape[1]
    owned = segs // seq_count
    past_start = lax.broadcasted_iota(jnp.int32, (wide, segs), 0) - bounds[:1, :].astype(jnp.int32)
    to_end = (sizes[:1, :].astype(jnp.int32) - 1 - past_start).astype(jnp.int16)
    past_start = past_start.astype(jnp.int16)
    one, zero = jnp.ones((wide, segs), bf16), jnp.zeros((wide, segs), bf16)
    sums = [jnp.zeros((2 * group, segs), f32) for _ in range(ACC)]
    arrived, leaving = order_of(OUT_ORDER, seq_count), order_of(BACK_ORDER, seq_count)
    for at, device in enumerate(arrived):
        for step in range(subs // 2):
            halves = []
            for sub in (2 * step, 2 * step + 1):
                base = at * (subs * group + 1) + sub * group
                from_row = at * per + (sub * 3 + 2) * group
                mixed = conv[base : base + group, :] * taken[from_row : from_row + group, :]
                out[leaving.index(device), sub * group : (sub + 1) * group, :] = mixed
                halves.append(mixed)
            hi, lo = split(jnp.concatenate(halves, 1))
            offset = (device * subs + 2 * step) * LANES
            member = jnp.where(
                (past_start >= jnp.int16(-offset)) & (to_end >= jnp.int16(offset)), one, zero
            )
            which = (at * (subs // 2) + step) % ACC
            sums[which] = sums[which] + mm(jnp.concatenate([hi, lo], 0), member)
    acc = sum(sums[1:], sums[0])
    pooled = (acc[:group] + acc[group:]) / sizes[:group, :]
    pooled = jnp.concatenate([pooled, jnp.zeros((LANES - group, segs), f32)], 0).T
    shift = lax.rem(place_in(arrived), LANES // group) * group
    pooled = pltpu.roll(pooled, shift, 1)
    for at, device in enumerate(leaving):
        out[at, subs * group :, :] = pooled[device * owned : (device + 1) * owned, :]


def back_kernel(taken, mixed, pooled, *, seq_count, group, subs):
    channels = seq_count * group
    leaving = order_of(BACK_ORDER, seq_count)
    holder = [leaving.index(device) for device in order_of(OUT_ORDER, seq_count)]
    for sub in range(subs):
        block = jnp.concatenate([taken[at, sub * group : (sub + 1) * group, :] for at in holder], 0)
        mixed[sub * LANES : (sub + 1) * LANES, :] = block.T
    per_lane = LANES // group
    for half in range(channels // LANES):
        total = taken[holder[half * per_lane], subs * group :, :]
        for at in holder[half * per_lane + 1 : (half + 1) * per_lane]:
            total = total + taken[at, subs * group :, :]
        pooled[:, half * LANES : (half + 1) * LANES] = total


def in_vmem(value):
    return pltpu.with_memory_space_constraint(value, pltpu.VMEM)


def on_device(signal, filter_taps, out_gate, skip_gain, lengths, row_of_segment):
    seq_count = lax.axis_size("seq")
    block_rows, channels = signal.shape
    group = channels // seq_count
    subs = block_rows // LANES
    segs = lengths.shape[0]
    owned = segs // seq_count
    sizes = dict(seq_count=seq_count, group=group, subs=subs)
    anywhere = pl.BlockSpec(memory_space=pltpu.HBM)
    consts = jnp.asarray(tables(seq_count, subs))
    sent, bounds, row_sizes, table = pl.pallas_call(
        functools.partial(turn_kernel, **sizes),
        in_specs=[anywhere] * 7,
        out_shape=(
            pltpu.VMEM((seq_count, 3 * subs * group, LANES), f32),
            pltpu.VMEM((2 * group, segs), f32),
            pltpu.VMEM((2 * group, segs), f32),
            pltpu.VMEM(consts.shape, bf16),
        ),
        scratch_shapes=[
            pltpu.VMEM((3, subs * LANES, channels), f32),
            pltpu.VMEM((1, channels), f32),
            pltpu.VMEM((2, 1, segs), jnp.int32),
            pltpu.SemaphoreType.DMA((3 * subs,)),
            pltpu.SemaphoreType.DMA((4,)),
        ],
        interpret=INTERPRET,
        name="turn",
        compiler_params=pltpu.CompilerParams(vmem_limit_bytes=VMEM_LIMIT),
    )(
        *(
            pltpu.with_memory_space_constraint(value, pltpu.HBM)
            for value in (
                signal,
                filter_taps,
                out_gate,
                skip_gain.reshape(1, channels),
                lengths.reshape(1, segs),
                row_of_segment.reshape(1, segs),
                consts,
            )
        )
    )
    taken = exchange(sent, order_of(OUT_ORDER, seq_count))
    taken = in_vmem(taken.reshape(seq_count * 3 * subs * group, LANES))
    mixed_sent = pl.pallas_call(
        functools.partial(conv_kernel, **sizes),
        out_shape=pltpu.VMEM((seq_count, subs * group + owned, LANES), f32),
        scratch_shapes=[
            pltpu.VMEM((seq_count * (subs * group + 1), LANES), f32),
            pltpu.VMEM((2 * group * seq_count * subs, 4 * LANES), bf16),
            pltpu.VMEM((group * seq_count * subs, 4 * LANES), bf16),
            pltpu.VMEM((2 * group * seq_count * subs, 2 * LANES), bf16),
            pltpu.VMEM((seq_count * (2 * subs * group + 1), LANES), f32),
        ],
        interpret=INTERPRET,
        name="conv",
        compiler_params=pltpu.CompilerParams(vmem_limit_bytes=VMEM_LIMIT),
    )(taken, in_vmem(bounds), in_vmem(row_sizes), in_vmem(table))
    back = exchange(mixed_sent, order_of(BACK_ORDER, seq_count))
    back = in_vmem(back)
    return pl.pallas_call(
        functools.partial(back_kernel, **sizes),
        out_shape=(
            jax.ShapeDtypeStruct((block_rows, channels), f32),
            jax.ShapeDtypeStruct((owned, channels), f32),
        ),
        interpret=INTERPRET,
        name="back",
        compiler_params=pltpu.CompilerParams(vmem_limit_bytes=VMEM_LIMIT),
    )(back)


def solution(mesh):
    placed = (P("seq", "chan"), P("seq", "chan"), P("seq", "chan"), P("chan"), P(), P())
    return jax.shard_map(
        on_device,
        mesh=mesh,
        in_specs=placed,
        out_specs=(P("seq", "chan"), P("seq", "chan")),
        check_vma=False,
    )
```

```python
import functools
import math

import jax
import jax.numpy as jnp
import numpy as np
from jax import lax
from jax.experimental import pallas as pl
from jax.experimental.pallas import tpu as pltpu
from jax.sharding import PartitionSpec as P


LANES = 128
VMEM_LIMIT = 24 << 20
FWD = 8
ACC = 2
INV = 4
INTERPRET = False
OUT_ORDER = [10, 11, 5, 2, 7, 4, 12, 9, 8, 3, 1, 14, 13, 0, 15, 6]
BACK_ORDER = OUT_ORDER
bf16 = jnp.bfloat16
f32 = jnp.float32


def order_of(wanted, seq_count):
    return wanted if len(wanted) == seq_count else list(range(seq_count))


def exchange(value, order):
    return lax.all_to_all(value, "seq", 0, 0, axis_index_groups=[order])


def place_in(order):
    mine = lax.axis_index("seq")
    place = jnp.int32(0)
    for at, device in enumerate(order):
        place = jnp.where(mine == device, at, place)
    return place


def split_const(value):
    hi = value.astype(bf16)
    return hi, (value - hi.astype(np.float64)).astype(bf16)


@functools.lru_cache(None)
def tables(seq_count, subs):
    rows = seq_count * subs
    total = rows * LANES
    order = order_of(OUT_ORDER, seq_count)
    t1 = np.array([device * subs + sub for sub in range(subs) for device in order], np.float64)
    k1 = np.arange(rows, dtype=np.float64)
    t2 = np.arange(LANES, dtype=np.float64)
    first = -2.0 * math.pi * (k1[:, None] + 0.25) * t1[None, :] / rows
    hi, lo = split_const(np.concatenate([np.cos(first), np.sin(first)], 0))
    first3 = np.concatenate([hi, lo, hi, np.zeros_like(hi)], 1)
    angle = 2.0 * math.pi * (np.outer(t2, t2) % LANES) / LANES
    cos, sin = np.cos(angle), np.sin(angle)
    forward = np.block([[cos, -sin], [sin, cos]])
    last = 2.0 * math.pi * t1[:, None] * (k1[None, :] + 0.25) / rows
    last_hi, last_lo = split_const(np.concatenate([np.cos(last), np.sin(last)], 1) / total)
    twist = -2.0 * math.pi * (k1[:, None] + 0.25) * t2[None, :] / total
    twist = np.concatenate([np.cos(twist), np.sin(twist)], 1)
    high, middle = split_const(twist)
    low = (twist - high.astype(np.float64) - middle.astype(np.float64)).astype(bf16)
    parts = [
        *split_const(forward),
        first3,
        np.concatenate([last_hi, last_lo], 1),
        np.concatenate([last_hi, np.zeros_like(last_hi)], 1),
        high,
        middle,
        low,
    ]
    return np.concatenate(parts, 0)


def split(value):
    hi = value.astype(bf16)
    lo = (value - hi.astype(f32)).astype(bf16)
    return hi, lo


def mm(left, right):
    return lax.dot_general(left, right, (((1,), (0,)), ((), ())), preferred_element_type=f32)


def turn_kernel(
    signal, taps, gate, skip, lengths, row_of, consts, out, bounds, sizes, table,
    big, row, ints, sems, small_sems,
    *, seq_count, group, subs
):
    small = (
        pltpu.make_async_copy(lengths, ints.at[0], small_sems.at[0]),
        pltpu.make_async_copy(row_of, ints.at[1], small_sems.at[1]),
        pltpu.make_async_copy(skip, row, small_sems.at[2]),
    )
    for copy in small:
        copy.start()
    constant = pltpu.make_async_copy(consts, table, small_sems.at[3])
    large = []
    for which, ref in enumerate((signal, taps, gate)):
        large.append(pltpu.make_async_copy(ref, big.at[which], sems.at[which]))
        large[-1].start()
    constant.start()
    for copy in small:
        copy.wait()

    segs = ints.shape[2]
    seg_len = jnp.broadcast_to(ints[0].astype(f32), (segs, segs)).T
    seg_row = jnp.broadcast_to(ints[1].astype(f32), (segs, segs)).T
    seg_at = lax.broadcasted_iota(jnp.int32, (segs, segs), 0).astype(f32)
    hit = seg_row == lax.broadcasted_iota(jnp.int32, (segs, segs), 1).astype(f32)
    which_seg = jnp.sum(jnp.where(hit, seg_at, 0.0), axis=0, keepdims=True)
    row_len = jnp.sum(jnp.where(hit, seg_len, 0.0), axis=0, keepdims=True)
    row_start = jnp.sum(jnp.where(seg_at < which_seg, seg_len, 0.0), axis=0, keepdims=True)
    bounds[...] = jnp.broadcast_to(row_start, bounds.shape)
    sizes[...] = jnp.broadcast_to(row_len, sizes.shape)

    at_start = lax.axis_index("seq") == 0
    for which in range(3):
        large[which].wait()
        for sub in range(subs):
            value = big[which, sub * LANES : (sub + 1) * LANES, :]
            if which == 1 and sub == 0:
                place = lax.broadcasted_iota(jnp.int32, value.shape, 0)
                value = value + jnp.where((place == 0) & at_start, row[...], 0.0)
            base = (sub * 3 + which) * group
            out[:, base : base + group, :] = value.T.reshape(seq_count, group, LANES)
    constant.wait()


def conv_kernel(
    taken, bounds, sizes, table, out, conv, turned, product, unturned, spread, *, seq_count, group, subs
):
    rows = seq_count * subs
    per = 3 * subs * group
    wide = 2 * LANES

    def tabled(at, count, lanes=wide):
        return table[at : at + count, :lanes]

    at = 2 * wide
    first3 = tabled(at, 2 * rows, 3 * rows)
    at += 2 * rows
    last3 = jnp.concatenate([tabled(at, rows), tabled(at + rows, rows, LANES)], 1)
    at += 2 * rows
    twist = tabled(at, rows).astype(f32) + tabled(at + rows, rows).astype(f32)
    twist = twist + tabled(at + 2 * rows, rows).astype(f32)
    twist_re, twist_im = twist[:, :LANES], twist[:, LANES:]

    pitch = 2 * subs * group + 1
    for device in range(seq_count):
        for sub in range(subs):
            for which in range(2):
                base = device * pitch + (sub * 2 + which) * group
                from_row = device * per + (sub * 3 + which) * group
                spread[base : base + group, :] = taken[from_row : from_row + group, :]

    def gather(which, channel):
        parts = []
        for sub in range(subs):
            start = (sub * 2 + which) * group + channel
            parts.append(spread[pl.ds(start, seq_count, stride=pitch), :])
        return jnp.concatenate(parts, 0)

    for channel in range(group):
        both = jnp.concatenate([gather(0, channel), gather(1, channel)], 1)
        hi, lo = split(both)
        stage = mm(first3, jnp.concatenate([hi, hi, lo], 0))
        for side in range(2):
            lanes = slice(side * LANES, (side + 1) * LANES)
            re, im = stage[:rows, lanes], stage[rows:, lanes]
            at = slice((2 * channel + side) * rows, (2 * channel + side + 1) * rows)
            for half, value in enumerate((re * twist_re - im * twist_im, re * twist_im + im * twist_re)):
                lanes_out = slice(half * LANES, (half + 1) * LANES)
                hi, lo = split(value)
                turned[at, lanes_out] = hi
                turned[at, 2 * LANES + half * LANES : 2 * LANES + (half + 1) * LANES] = lo

    def three(ref, at):
        high, low = tabled(0, wide), tabled(wide, wide)
        return mm(jnp.concatenate([ref[at, :], ref[at, :wide]], 1), jnp.concatenate([high, high, low], 0))

    for block in range(group // FWD):
        spec = three(turned, slice(block * FWD * 2 * rows, (block + 1) * FWD * 2 * rows))
        for at in range(FWD):
            channel = block * FWD + at
            left = spec[(2 * at) * rows : (2 * at + 1) * rows]
            right = spec[(2 * at + 1) * rows : (2 * at + 2) * rows]
            left_re, left_im = left[:, :LANES], left[:, LANES:]
            right_re, right_im = right[:, :LANES], right[:, LANES:]
            products = (left_re * right_re - left_im * right_im, -(left_re * right_im) - left_im * right_re)
            here = slice(channel * rows, (channel + 1) * rows)
            for half, value in enumerate(products):
                hi, lo = split(value)
                product[here, half * LANES : (half + 1) * LANES] = hi
                product[here, (2 + half) * LANES : (3 + half) * LANES] = lo

    for block in range(group // INV):
        back = three(product, slice(block * INV * rows, (block + 1) * INV * rows))
        for at in range(INV):
            channel = block * INV + at
            lanes = slice(channel % 2 * LANES, (channel % 2 + 1) * LANES)
            re, im = back[at * rows : (at + 1) * rows, :LANES], back[at * rows : (at + 1) * rows, LANES:]
            values = (re * twist_re - im * twist_im, im * twist_re + re * twist_im)
            for half, value in enumerate(values):
                hi, lo = split(value)
                base = channel // 2 * 4 * rows + half * rows
                unturned[base : base + rows, lanes] = hi
                unturned[base + 2 * rows : base + 3 * rows, lanes] = lo

    for pair in range(group // 2):
        hi = unturned[pair * 4 * rows : pair * 4 * rows + 2 * rows, :]
        lo = unturned[pair * 4 * rows + 2 * rows : (pair + 1) * 4 * rows, :]
        result = mm(last3, jnp.concatenate([hi, hi, lo], 0))
        for at in range(2):
            for sub in range(subs):
                start = sub * group + pair * 2 + at
                conv[pl.ds(start, seq_count, stride=subs * group + 1), :] = result[
                    sub * seq_count : (sub + 1) * seq_count, at * LANES : (at + 1) * LANES
                ]

    segs = sizes.shape[1]
    owned = segs // seq_count
    past_start = lax.broadcasted_iota(jnp.int32, (wide, segs), 0) - bounds[:1, :].astype(jnp.int32)
    to_end = (sizes[:1, :].astype(jnp.int32) - 1 - past_start).astype(jnp.int16)
    past_start = past_start.astype(jnp.int16)
    one, zero = jnp.ones((wide, segs), bf16), jnp.zeros((wide, segs), bf16)
    sums = [jnp.zeros((2 * group, segs), f32) for _ in range(ACC)]
    arrived, leaving = order_of(OUT_ORDER, seq_count), order_of(BACK_ORDER, seq_count)
    for at, device in enumerate(arrived):
        for step in range(subs // 2):
            halves = []
            for sub in (2 * step, 2 * step + 1):
                base = at * (subs * group + 1) + sub * group
                from_row = at * per + (sub * 3 + 2) * group
                mixed = conv[base : base + group, :] * taken[from_row : from_row + group, :]
                out[leaving.index(device), sub * group : (sub + 1) * group, :] = mixed
                halves.append(mixed)
            hi, lo = split(jnp.concatenate(halves, 1))
            offset = (device * subs + 2 * step) * LANES
            member = jnp.where(
                (past_start >= jnp.int16(-offset)) & (to_end >= jnp.int16(offset)), one, zero
            )
            which = (at * (subs // 2) + step) % ACC
            sums[which] = sums[which] + mm(jnp.concatenate([hi, lo], 0), member)
    acc = sum(sums[1:], sums[0])
    pooled = (acc[:group] + acc[group:]) / sizes[:group, :]
    pooled = jnp.concatenate([pooled, jnp.zeros((LANES - group, segs), f32)], 0).T
    shift = lax.rem(place_in(arrived), LANES // group) * group
    pooled = pltpu.roll(pooled, shift, 1)
    for at, device in enumerate(leaving):
        out[at, subs * group :, :] = pooled[device * owned : (device + 1) * owned, :]


def back_kernel(taken, mixed, pooled, turned, summed, sems, *, seq_count, group, subs):
    channels = seq_count * group
    leaving = order_of(BACK_ORDER, seq_count)
    holder = [leaving.index(device) for device in order_of(OUT_ORDER, seq_count)]
    copies = []
    for sub in range(subs):
        block = jnp.concatenate([taken[at, sub * group : (sub + 1) * group, :] for at in holder], 0)
        turned[sub] = block.T
        rows = pl.ds(sub * LANES, LANES)
        copies.append(pltpu.make_async_copy(turned.at[sub], mixed.at[rows, :], sems.at[sub]))
        copies[-1].start()
    per_lane = LANES // group
    for half in range(channels // LANES):
        total = taken[holder[half * per_lane], subs * group :, :]
        for at in holder[half * per_lane + 1 : (half + 1) * per_lane]:
            total = total + taken[at, subs * group :, :]
        summed[:, half * LANES : (half + 1) * LANES] = total
    copies.append(pltpu.make_async_copy(summed, pooled, sems.at[subs]))
    copies[-1].start()
    for copy in copies:
        copy.wait()


def in_vmem(value):
    return pltpu.with_memory_space_constraint(value, pltpu.VMEM)


def on_device(signal, filter_taps, out_gate, skip_gain, lengths, row_of_segment):
    seq_count = lax.axis_size("seq")
    block_rows, channels = signal.shape
    group = channels // seq_count
    subs = block_rows // LANES
    segs = lengths.shape[0]
    owned = segs // seq_count
    sizes = dict(seq_count=seq_count, group=group, subs=subs)
    anywhere = pl.BlockSpec(memory_space=pltpu.HBM)
    consts = jnp.asarray(tables(seq_count, subs))
    sent, bounds, row_sizes, table = pl.pallas_call(
        functools.partial(turn_kernel, **sizes),
        in_specs=[anywhere] * 7,
        out_shape=(
            pltpu.VMEM((seq_count, 3 * subs * group, LANES), f32),
            pltpu.VMEM((2 * group, segs), f32),
            pltpu.VMEM((2 * group, segs), f32),
            pltpu.VMEM(consts.shape, bf16),
        ),
        scratch_shapes=[
            pltpu.VMEM((3, subs * LANES, channels), f32),
            pltpu.VMEM((1, channels), f32),
            pltpu.VMEM((2, 1, segs), jnp.int32),
            pltpu.SemaphoreType.DMA((3 * subs,)),
            pltpu.SemaphoreType.DMA((4,)),
        ],
        interpret=INTERPRET,
        name="turn",
        compiler_params=pltpu.CompilerParams(vmem_limit_bytes=VMEM_LIMIT),
    )(
        *(
            pltpu.with_memory_space_constraint(value, pltpu.HBM)
            for value in (
                signal,
                filter_taps,
                out_gate,
                skip_gain.reshape(1, channels),
                lengths.reshape(1, segs),
                row_of_segment.reshape(1, segs),
                consts,
            )
        )
    )
    taken = exchange(sent, order_of(OUT_ORDER, seq_count))
    taken = in_vmem(taken.reshape(seq_count * 3 * subs * group, LANES))
    mixed_sent = pl.pallas_call(
        functools.partial(conv_kernel, **sizes),
        out_shape=pltpu.VMEM((seq_count, subs * group + owned, LANES), f32),
        scratch_shapes=[
            pltpu.VMEM((seq_count * (subs * group + 1), LANES), f32),
            pltpu.VMEM((2 * group * seq_count * subs, 4 * LANES), bf16),
            pltpu.VMEM((group * seq_count * subs, 4 * LANES), bf16),
            pltpu.VMEM((2 * group * seq_count * subs, 2 * LANES), bf16),
            pltpu.VMEM((seq_count * (2 * subs * group + 1), LANES), f32),
        ],
        interpret=INTERPRET,
        name="conv",
        compiler_params=pltpu.CompilerParams(vmem_limit_bytes=VMEM_LIMIT),
    )(taken, in_vmem(bounds), in_vmem(row_sizes), in_vmem(table))
    back = exchange(mixed_sent, order_of(BACK_ORDER, seq_count))
    back = in_vmem(back)
    return pl.pallas_call(
        functools.partial(back_kernel, **sizes),
        out_shape=(
            jax.ShapeDtypeStruct((block_rows, channels), f32),
            jax.ShapeDtypeStruct((owned, channels), f32),
        ),
        out_specs=(pl.BlockSpec(memory_space=pltpu.HBM), pl.BlockSpec(memory_space=pltpu.HBM)),
        scratch_shapes=[
            pltpu.VMEM((subs, LANES, channels), f32),
            pltpu.VMEM((owned, channels), f32),
            pltpu.SemaphoreType.DMA((subs + 1,)),
        ],
        interpret=INTERPRET,
        name="back",
        compiler_params=pltpu.CompilerParams(vmem_limit_bytes=VMEM_LIMIT),
    )(back)


def solution(mesh):
    placed = (P("seq", "chan"), P("seq", "chan"), P("seq", "chan"), P("chan"), P(), P())
    return jax.shard_map(
        on_device,
        mesh=mesh,
        in_specs=placed,
        out_specs=(P("seq", "chan"), P("seq", "chan")),
        check_vma=False,
    )
```

```python
import functools
import math

import jax
import jax.numpy as jnp
import numpy as np
from jax import lax
from jax.experimental import pallas as pl
from jax.experimental.pallas import tpu as pltpu
from jax.sharding import PartitionSpec as P


LANES = 128
VMEM_LIMIT = 24 << 20
FWD = 8
ACC = 2
INV = 4
INTERPRET = False
OUT_ORDER = [10, 11, 5, 2, 7, 4, 12, 9, 8, 3, 1, 14, 13, 0, 15, 6]
BACK_ORDER = OUT_ORDER
bf16 = jnp.bfloat16
f32 = jnp.float32


def order_of(wanted, seq_count):
    return wanted if len(wanted) == seq_count else list(range(seq_count))


def exchange(value, order):
    return lax.all_to_all(value, "seq", 0, 0, axis_index_groups=[order])


def place_in(order):
    mine = lax.axis_index("seq")
    place = jnp.int32(0)
    for at, device in enumerate(order):
        place = jnp.where(mine == device, at, place)
    return place


def split_const(value):
    hi = value.astype(bf16)
    return hi, (value - hi.astype(np.float64)).astype(bf16)


@functools.lru_cache(None)
def tables(seq_count, subs):
    rows = seq_count * subs
    total = rows * LANES
    order = order_of(OUT_ORDER, seq_count)
    t1 = np.array([device * subs + sub for sub in range(subs) for device in order], np.float64)
    k1 = np.arange(rows, dtype=np.float64)
    t2 = np.arange(LANES, dtype=np.float64)
    first = -2.0 * math.pi * (k1[:, None] + 0.25) * t1[None, :] / rows
    hi, lo = split_const(np.concatenate([np.cos(first), np.sin(first)], 0))
    first3 = np.concatenate([hi, lo, hi, np.zeros_like(hi)], 1)
    angle = 2.0 * math.pi * (np.outer(t2, t2) % LANES) / LANES
    cos, sin = np.cos(angle), np.sin(angle)
    forward = np.block([[cos, -sin], [sin, cos]])
    last = 2.0 * math.pi * t1[:, None] * (k1[None, :] + 0.25) / rows
    last_hi, last_lo = split_const(np.concatenate([np.cos(last), np.sin(last)], 1) / total)
    twist = -2.0 * math.pi * (k1[:, None] + 0.25) * t2[None, :] / total
    twist = np.concatenate([np.cos(twist), np.sin(twist)], 1)
    high, middle = split_const(twist)
    low = (twist - high.astype(np.float64) - middle.astype(np.float64)).astype(bf16)
    parts = [
        *split_const(forward),
        first3,
        np.concatenate([last_hi, last_lo], 1),
        np.concatenate([last_hi, np.zeros_like(last_hi)], 1),
        high,
        middle,
        low,
    ]
    return np.concatenate(parts, 0)


def split(value):
    hi = value.astype(bf16)
    lo = (value - hi.astype(f32)).astype(bf16)
    return hi, lo


def mm(left, right):
    return lax.dot_general(left, right, (((1,), (0,)), ((), ())), preferred_element_type=f32)


def turn_kernel(
    signal, taps, gate, skip, lengths, row_of, consts, out, bounds, sizes, table,
    big, row, ints, sems, small_sems,
    *, seq_count, group, subs
):
    small = (
        pltpu.make_async_copy(lengths, ints.at[0], small_sems.at[0]),
        pltpu.make_async_copy(row_of, ints.at[1], small_sems.at[1]),
        pltpu.make_async_copy(skip, row, small_sems.at[2]),
    )
    constant = pltpu.make_async_copy(consts, table, small_sems.at[3])
    large = []
    for which, ref in enumerate((signal, taps, gate)):
        large.append(pltpu.make_async_copy(ref, big.at[which], sems.at[which]))
        large[-1].start()
    for copy in small:
        copy.start()
    constant.start()
    for copy in small:
        copy.wait()

    segs = ints.shape[2]
    seg_len = jnp.broadcast_to(ints[0].astype(f32), (segs, segs)).T
    seg_row = jnp.broadcast_to(ints[1].astype(f32), (segs, segs)).T
    seg_at = lax.broadcasted_iota(jnp.int32, (segs, segs), 0).astype(f32)
    hit = seg_row == lax.broadcasted_iota(jnp.int32, (segs, segs), 1).astype(f32)
    which_seg = jnp.sum(jnp.where(hit, seg_at, 0.0), axis=0, keepdims=True)
    row_len = jnp.sum(jnp.where(hit, seg_len, 0.0), axis=0, keepdims=True)
    row_start = jnp.sum(jnp.where(seg_at < which_seg, seg_len, 0.0), axis=0, keepdims=True)
    bounds[...] = jnp.broadcast_to(row_start, bounds.shape)
    sizes[...] = jnp.broadcast_to(row_len, sizes.shape)

    at_start = lax.axis_index("seq") == 0
    for which in range(3):
        large[which].wait()
        for sub in range(subs):
            value = big[which, sub * LANES : (sub + 1) * LANES, :]
            if which == 1 and sub == 0:
                place = lax.broadcasted_iota(jnp.int32, value.shape, 0)
                value = value + jnp.where((place == 0) & at_start, row[...], 0.0)
            base = (sub * 3 + which) * group
            out[:, base : base + group, :] = value.T.reshape(seq_count, group, LANES)
    constant.wait()


def conv_kernel(
    taken, bounds, sizes, table, out, conv, turned, product, unturned, spread, *, seq_count, group, subs
):
    rows = seq_count * subs
    per = 3 * subs * group
    wide = 2 * LANES

    def tabled(at, count, lanes=wide):
        return table[at : at + count, :lanes]

    at = 2 * wide
    first3 = tabled(at, 2 * rows, 3 * rows)
    at += 2 * rows
    last3 = jnp.concatenate([tabled(at, rows), tabled(at + rows, rows, LANES)], 1)
    at += 2 * rows
    twist = tabled(at, rows).astype(f32) + tabled(at + rows, rows).astype(f32)
    twist = twist + tabled(at + 2 * rows, rows).astype(f32)
    twist_re, twist_im = twist[:, :LANES], twist[:, LANES:]

    pitch = 2 * subs * group + 1
    for device in range(seq_count):
        for sub in range(subs):
            for which in range(2):
                base = device * pitch + (sub * 2 + which) * group
                from_row = device * per + (sub * 3 + which) * group
                spread[base : base + group, :] = taken[from_row : from_row + group, :]

    def gather(which, channel):
        parts = []
        for sub in range(subs):
            start = (sub * 2 + which) * group + channel
            parts.append(spread[pl.ds(start, seq_count, stride=pitch), :])
        return jnp.concatenate(parts, 0)

    for channel in range(group):
        both = jnp.concatenate([gather(0, channel), gather(1, channel)], 1)
        hi, lo = split(both)
        stage = mm(first3, jnp.concatenate([hi, hi, lo], 0))
        for side in range(2):
            lanes = slice(side * LANES, (side + 1) * LANES)
            re, im = stage[:rows, lanes], stage[rows:, lanes]
            at = slice((2 * channel + side) * rows, (2 * channel + side + 1) * rows)
            for half, value in enumerate((re * twist_re - im * twist_im, re * twist_im + im * twist_re)):
                lanes_out = slice(half * LANES, (half + 1) * LANES)
                hi, lo = split(value)
                turned[at, lanes_out] = hi
                turned[at, 2 * LANES + half * LANES : 2 * LANES + (half + 1) * LANES] = lo

    def three(ref, at):
        high, low = tabled(0, wide), tabled(wide, wide)
        return mm(jnp.concatenate([ref[at, :], ref[at, :wide]], 1), jnp.concatenate([high, high, low], 0))

    for block in range(group // FWD):
        spec = three(turned, slice(block * FWD * 2 * rows, (block + 1) * FWD * 2 * rows))
        for at in range(FWD):
            channel = block * FWD + at
            left = spec[(2 * at) * rows : (2 * at + 1) * rows]
            right = spec[(2 * at + 1) * rows : (2 * at + 2) * rows]
            left_re, left_im = left[:, :LANES], left[:, LANES:]
            right_re, right_im = right[:, :LANES], right[:, LANES:]
            products = (left_re * right_re - left_im * right_im, -(left_re * right_im) - left_im * right_re)
            here = slice(channel * rows, (channel + 1) * rows)
            for half, value in enumerate(products):
                hi, lo = split(value)
                product[here, half * LANES : (half + 1) * LANES] = hi
                product[here, (2 + half) * LANES : (3 + half) * LANES] = lo

    for block in range(group // INV):
        back = three(product, slice(block * INV * rows, (block + 1) * INV * rows))
        for at in range(INV):
            channel = block * INV + at
            lanes = slice(channel % 2 * LANES, (channel % 2 + 1) * LANES)
            re, im = back[at * rows : (at + 1) * rows, :LANES], back[at * rows : (at + 1) * rows, LANES:]
            values = (re * twist_re - im * twist_im, im * twist_re + re * twist_im)
            for half, value in enumerate(values):
                hi, lo = split(value)
                base = channel // 2 * 4 * rows + half * rows
                unturned[base : base + rows, lanes] = hi
                unturned[base + 2 * rows : base + 3 * rows, lanes] = lo

    for pair in range(group // 2):
        hi = unturned[pair * 4 * rows : pair * 4 * rows + 2 * rows, :]
        lo = unturned[pair * 4 * rows + 2 * rows : (pair + 1) * 4 * rows, :]
        result = mm(last3, jnp.concatenate([hi, hi, lo], 0))
        for at in range(2):
            for sub in range(subs):
                start = sub * group + pair * 2 + at
                conv[pl.ds(start, seq_count, stride=subs * group + 1), :] = result[
                    sub * seq_count : (sub + 1) * seq_count, at * LANES : (at + 1) * LANES
                ]

    segs = sizes.shape[1]
    owned = segs // seq_count
    past_start = lax.broadcasted_iota(jnp.int32, (wide, segs), 0) - bounds[:1, :].astype(jnp.int32)
    to_end = (sizes[:1, :].astype(jnp.int32) - 1 - past_start).astype(jnp.int16)
    past_start = past_start.astype(jnp.int16)
    one, zero = jnp.ones((wide, segs), bf16), jnp.zeros((wide, segs), bf16)
    sums = [jnp.zeros((2 * group, segs), f32) for _ in range(ACC)]
    arrived, leaving = order_of(OUT_ORDER, seq_count), order_of(BACK_ORDER, seq_count)
    for at, device in enumerate(arrived):
        for step in range(subs // 2):
            halves = []
            for sub in (2 * step, 2 * step + 1):
                base = at * (subs * group + 1) + sub * group
                from_row = at * per + (sub * 3 + 2) * group
                mixed = conv[base : base + group, :] * taken[from_row : from_row + group, :]
                out[leaving.index(device), sub * group : (sub + 1) * group, :] = mixed
                halves.append(mixed)
            hi, lo = split(jnp.concatenate(halves, 1))
            offset = (device * subs + 2 * step) * LANES
            member = jnp.where(
                (past_start >= jnp.int16(-offset)) & (to_end >= jnp.int16(offset)), one, zero
            )
            which = (at * (subs // 2) + step) % ACC
            sums[which] = sums[which] + mm(jnp.concatenate([hi, lo], 0), member)
    acc = sum(sums[1:], sums[0])
    pooled = (acc[:group] + acc[group:]) / sizes[:group, :]
    pooled = jnp.concatenate([pooled, jnp.zeros((LANES - group, segs), f32)], 0).T
    shift = lax.rem(place_in(arrived), LANES // group) * group
    pooled = pltpu.roll(pooled, shift, 1)
    for at, device in enumerate(leaving):
        out[at, subs * group :, :] = pooled[device * owned : (device + 1) * owned, :]


def back_kernel(taken, mixed, pooled, turned, summed, sems, *, seq_count, group, subs):
    channels = seq_count * group
    leaving = order_of(BACK_ORDER, seq_count)
    holder = [leaving.index(device) for device in order_of(OUT_ORDER, seq_count)]
    copies = []
    for sub in range(subs):
        block = jnp.concatenate([taken[at, sub * group : (sub + 1) * group, :] for at in holder], 0)
        turned[sub] = block.T
        rows = pl.ds(sub * LANES, LANES)
        copies.append(pltpu.make_async_copy(turned.at[sub], mixed.at[rows, :], sems.at[sub]))
        copies[-1].start()
    per_lane = LANES // group
    for half in range(channels // LANES):
        total = taken[holder[half * per_lane], subs * group :, :]
        for at in holder[half * per_lane + 1 : (half + 1) * per_lane]:
            total = total + taken[at, subs * group :, :]
        summed[:, half * LANES : (half + 1) * LANES] = total
    copies.append(pltpu.make_async_copy(summed, pooled, sems.at[subs]))
    copies[-1].start()
    for copy in copies:
        copy.wait()


def in_vmem(value):
    return pltpu.with_memory_space_constraint(value, pltpu.VMEM)


def on_device(signal, filter_taps, out_gate, skip_gain, lengths, row_of_segment):
    seq_count = lax.axis_size("seq")
    block_rows, channels = signal.shape
    group = channels // seq_count
    subs = block_rows // LANES
    segs = lengths.shape[0]
    owned = segs // seq_count
    sizes = dict(seq_count=seq_count, group=group, subs=subs)
    anywhere = pl.BlockSpec(memory_space=pltpu.HBM)
    consts = jnp.asarray(tables(seq_count, subs))
    sent, bounds, row_sizes, table = pl.pallas_call(
        functools.partial(turn_kernel, **sizes),
        in_specs=[anywhere] * 7,
        out_shape=(
            pltpu.VMEM((seq_count, 3 * subs * group, LANES), f32),
            pltpu.VMEM((2 * group, segs), f32),
            pltpu.VMEM((2 * group, segs), f32),
            pltpu.VMEM(consts.shape, bf16),
        ),
        scratch_shapes=[
            pltpu.VMEM((3, subs * LANES, channels), f32),
            pltpu.VMEM((1, channels), f32),
            pltpu.VMEM((2, 1, segs), jnp.int32),
            pltpu.SemaphoreType.DMA((3 * subs,)),
            pltpu.SemaphoreType.DMA((4,)),
        ],
        interpret=INTERPRET,
        name="turn",
        compiler_params=pltpu.CompilerParams(vmem_limit_bytes=VMEM_LIMIT),
    )(
        *(
            pltpu.with_memory_space_constraint(value, pltpu.HBM)
            for value in (
                signal,
                filter_taps,
                out_gate,
                skip_gain.reshape(1, channels),
                lengths.reshape(1, segs),
                row_of_segment.reshape(1, segs),
                consts,
            )
        )
    )
    taken = exchange(sent, order_of(OUT_ORDER, seq_count))
    taken = in_vmem(taken.reshape(seq_count * 3 * subs * group, LANES))
    mixed_sent = pl.pallas_call(
        functools.partial(conv_kernel, **sizes),
        out_shape=pltpu.VMEM((seq_count, subs * group + owned, LANES), f32),
        scratch_shapes=[
            pltpu.VMEM((seq_count * (subs * group + 1), LANES), f32),
            pltpu.VMEM((2 * group * seq_count * subs, 4 * LANES), bf16),
            pltpu.VMEM((group * seq_count * subs, 4 * LANES), bf16),
            pltpu.VMEM((2 * group * seq_count * subs, 2 * LANES), bf16),
            pltpu.VMEM((seq_count * (2 * subs * group + 1), LANES), f32),
        ],
        interpret=INTERPRET,
        name="conv",
        compiler_params=pltpu.CompilerParams(vmem_limit_bytes=VMEM_LIMIT),
    )(taken, in_vmem(bounds), in_vmem(row_sizes), in_vmem(table))
    back = exchange(mixed_sent, order_of(BACK_ORDER, seq_count))
    back = in_vmem(back)
    return pl.pallas_call(
        functools.partial(back_kernel, **sizes),
        out_shape=(
            jax.ShapeDtypeStruct((block_rows, channels), f32),
            jax.ShapeDtypeStruct((owned, channels), f32),
        ),
        out_specs=(pl.BlockSpec(memory_space=pltpu.HBM), pl.BlockSpec(memory_space=pltpu.HBM)),
        scratch_shapes=[
            pltpu.VMEM((subs, LANES, channels), f32),
            pltpu.VMEM((owned, channels), f32),
            pltpu.SemaphoreType.DMA((subs + 1,)),
        ],
        interpret=INTERPRET,
        name="back",
        compiler_params=pltpu.CompilerParams(vmem_limit_bytes=VMEM_LIMIT),
    )(back)


def solution(mesh):
    placed = (P("seq", "chan"), P("seq", "chan"), P("seq", "chan"), P("chan"), P(), P())
    return jax.shard_map(
        on_device,
        mesh=mesh,
        in_specs=placed,
        out_specs=(P("seq", "chan"), P("seq", "chan")),
        check_vma=False,
    )
```

```python
import functools
import math

import jax
import jax.numpy as jnp
import numpy as np
from jax import lax
from jax.experimental import pallas as pl
from jax.experimental.pallas import tpu as pltpu
from jax.sharding import PartitionSpec as P


LANES = 128
VMEM_LIMIT = 24 << 20
FWD = 8
ACC = 2
INV = 4
INTERPRET = False
OUT_ORDER = [10, 11, 5, 2, 7, 4, 12, 9, 8, 3, 1, 14, 13, 0, 15, 6]
BACK_ORDER = OUT_ORDER
bf16 = jnp.bfloat16
f32 = jnp.float32


def order_of(wanted, seq_count):
    return wanted if len(wanted) == seq_count else list(range(seq_count))


def exchange(value, order):
    return lax.all_to_all(value, "seq", 0, 0, axis_index_groups=[order])


def place_in(order):
    mine = lax.axis_index("seq")
    place = jnp.int32(0)
    for at, device in enumerate(order):
        place = jnp.where(mine == device, at, place)
    return place


def split_const(value):
    hi = value.astype(bf16)
    return hi, (value - hi.astype(np.float64)).astype(bf16)


@functools.lru_cache(None)
def tables(seq_count, subs):
    rows = seq_count * subs
    total = rows * LANES
    order = order_of(OUT_ORDER, seq_count)
    t1 = np.array([device * subs + sub for sub in range(subs) for device in order], np.float64)
    k1 = np.arange(rows, dtype=np.float64)
    t2 = np.arange(LANES, dtype=np.float64)
    first = -2.0 * math.pi * (k1[:, None] + 0.25) * t1[None, :] / rows
    hi, lo = split_const(np.concatenate([np.cos(first), np.sin(first)], 0))
    first3 = np.concatenate([hi, lo, hi, np.zeros_like(hi)], 1)
    angle = 2.0 * math.pi * (np.outer(t2, t2) % LANES) / LANES
    cos, sin = np.cos(angle), np.sin(angle)
    forward = np.block([[cos, -sin], [sin, cos]])
    last = 2.0 * math.pi * t1[:, None] * (k1[None, :] + 0.25) / rows
    last_hi, last_lo = split_const(np.concatenate([np.cos(last), np.sin(last)], 1) / total)
    twist = -2.0 * math.pi * (k1[:, None] + 0.25) * t2[None, :] / total
    twist = np.concatenate([np.cos(twist), np.sin(twist)], 1)
    high, middle = split_const(twist)
    low = (twist - high.astype(np.float64) - middle.astype(np.float64)).astype(bf16)
    parts = [
        *split_const(forward),
        first3,
        np.concatenate([last_hi, last_lo], 1),
        np.concatenate([last_hi, np.zeros_like(last_hi)], 1),
        high,
        middle,
        low,
    ]
    return np.concatenate(parts, 0)


def split(value):
    hi = value.astype(bf16)
    lo = (value - hi.astype(f32)).astype(bf16)
    return hi, lo


def mm(left, right):
    return lax.dot_general(left, right, (((1,), (0,)), ((), ())), preferred_element_type=f32)


def turn_kernel(
    signal, taps, gate, skip, lengths, row_of, consts, out, bounds, sizes, table,
    big, row, ints, sems, small_sems,
    *, seq_count, group, subs
):
    small = (
        pltpu.make_async_copy(lengths, ints.at[0], small_sems.at[0]),
        pltpu.make_async_copy(row_of, ints.at[1], small_sems.at[1]),
        pltpu.make_async_copy(skip, row, small_sems.at[2]),
    )
    constant = pltpu.make_async_copy(consts, table, small_sems.at[3])
    large = []
    for which, ref in enumerate((signal, taps, gate)):
        large.append(pltpu.make_async_copy(ref, big.at[which], sems.at[which]))
        large[-1].start()
    for copy in small:
        copy.start()
    constant.start()
    for copy in small:
        copy.wait()

    segs = ints.shape[2]
    seg_len = jnp.broadcast_to(ints[0].astype(f32), (segs, segs)).T
    seg_row = jnp.broadcast_to(ints[1].astype(f32), (segs, segs)).T
    seg_at = lax.broadcasted_iota(jnp.int32, (segs, segs), 0).astype(f32)
    hit = seg_row == lax.broadcasted_iota(jnp.int32, (segs, segs), 1).astype(f32)
    which_seg = jnp.sum(jnp.where(hit, seg_at, 0.0), axis=0, keepdims=True)
    row_len = jnp.sum(jnp.where(hit, seg_len, 0.0), axis=0, keepdims=True)
    row_start = jnp.sum(jnp.where(seg_at < which_seg, seg_len, 0.0), axis=0, keepdims=True)
    bounds[...] = jnp.broadcast_to(row_start, bounds.shape)
    sizes[...] = jnp.broadcast_to(row_len, sizes.shape)

    at_start = lax.axis_index("seq") == 0
    for which in range(3):
        large[which].wait()
        for sub in range(subs):
            value = big[which, sub * LANES : (sub + 1) * LANES, :]
            if which == 1 and sub == 0:
                place = lax.broadcasted_iota(jnp.int32, value.shape, 0)
                value = value + jnp.where((place == 0) & at_start, row[...], 0.0)
            base = (sub * 3 + which) * group
            out[:, base : base + group, :] = value.T.reshape(seq_count, group, LANES)
    constant.wait()


def conv_kernel(
    taken, bounds, sizes, table, out, conv, turned, product, unturned, spread, *, seq_count, group, subs
):
    rows = seq_count * subs
    per = 3 * subs * group
    wide = 2 * LANES

    def tabled(at, count, lanes=wide):
        return table[at : at + count, :lanes]

    at = 2 * wide
    first3 = tabled(at, 2 * rows, 3 * rows)
    at += 2 * rows
    last3 = jnp.concatenate([tabled(at, rows), tabled(at + rows, rows, LANES)], 1)
    at += 2 * rows
    twist = tabled(at, rows).astype(f32) + tabled(at + rows, rows).astype(f32)
    twist = twist + tabled(at + 2 * rows, rows).astype(f32)
    twist_re, twist_im = twist[:, :LANES], twist[:, LANES:]

    pitch = 2 * subs * group + 1
    for device in range(seq_count):
        for sub in range(subs):
            for which in range(2):
                base = device * pitch + (sub * 2 + which) * group
                from_row = device * per + (sub * 3 + which) * group
                spread[base : base + group, :] = taken[from_row : from_row + group, :]

    def gather(which, channel):
        parts = []
        for sub in range(subs):
            start = (sub * 2 + which) * group + channel
            parts.append(spread[pl.ds(start, seq_count, stride=pitch), :])
        return jnp.concatenate(parts, 0)

    for channel in range(group):
        both = jnp.concatenate([gather(0, channel), gather(1, channel)], 1)
        hi, lo = split(both)
        stage = mm(first3, jnp.concatenate([hi, hi, lo], 0))
        for side in range(2):
            lanes = slice(side * LANES, (side + 1) * LANES)
            re, im = stage[:rows, lanes], stage[rows:, lanes]
            at = slice((2 * channel + side) * rows, (2 * channel + side + 1) * rows)
            for half, value in enumerate((re * twist_re - im * twist_im, re * twist_im + im * twist_re)):
                lanes_out = slice(half * LANES, (half + 1) * LANES)
                hi, lo = split(value)
                turned[at, lanes_out] = hi
                turned[at, 2 * LANES + half * LANES : 2 * LANES + (half + 1) * LANES] = lo

    def three(ref, at):
        high, low = tabled(0, wide), tabled(wide, wide)
        return mm(jnp.concatenate([ref[at, :], ref[at, :wide]], 1), jnp.concatenate([high, high, low], 0))

    for block in range(group // FWD):
        spec = three(turned, slice(block * FWD * 2 * rows, (block + 1) * FWD * 2 * rows))
        for at in range(FWD):
            channel = block * FWD + at
            left = spec[(2 * at) * rows : (2 * at + 1) * rows]
            right = spec[(2 * at + 1) * rows : (2 * at + 2) * rows]
            left_re, left_im = left[:, :LANES], left[:, LANES:]
            right_re, right_im = right[:, :LANES], right[:, LANES:]
            products = (left_re * right_re - left_im * right_im, -(left_re * right_im) - left_im * right_re)
            here = slice(channel * rows, (channel + 1) * rows)
            for half, value in enumerate(products):
                hi, lo = split(value)
                product[here, half * LANES : (half + 1) * LANES] = hi
                product[here, (2 + half) * LANES : (3 + half) * LANES] = lo

    for block in range(group // INV):
        back = three(product, slice(block * INV * rows, (block + 1) * INV * rows))
        for at in range(INV):
            channel = block * INV + at
            lanes = slice(channel % 2 * LANES, (channel % 2 + 1) * LANES)
            re, im = back[at * rows : (at + 1) * rows, :LANES], back[at * rows : (at + 1) * rows, LANES:]
            values = (re * twist_re - im * twist_im, im * twist_re + re * twist_im)
            for half, value in enumerate(values):
                hi, lo = split(value)
                base = channel // 2 * 4 * rows + half * rows
                unturned[base : base + rows, lanes] = hi
                unturned[base + 2 * rows : base + 3 * rows, lanes] = lo

    for pair in range(group // 2):
        hi = unturned[pair * 4 * rows : pair * 4 * rows + 2 * rows, :]
        lo = unturned[pair * 4 * rows + 2 * rows : (pair + 1) * 4 * rows, :]
        result = mm(last3, jnp.concatenate([hi, hi, lo], 0))
        for at in range(2):
            for sub in range(subs):
                start = sub * group + pair * 2 + at
                conv[pl.ds(start, seq_count, stride=subs * group + 1), :] = result[
                    sub * seq_count : (sub + 1) * seq_count, at * LANES : (at + 1) * LANES
                ]

    segs = sizes.shape[1]
    owned = segs // seq_count
    past_start = lax.broadcasted_iota(jnp.int32, (wide, segs), 0) - bounds[:1, :].astype(jnp.int32)
    to_end = (sizes[:1, :].astype(jnp.int32) - 1 - past_start).astype(jnp.int16)
    past_start = past_start.astype(jnp.int16)
    one, zero = jnp.ones((wide, segs), bf16), jnp.zeros((wide, segs), bf16)
    sums = [jnp.zeros((2 * group, segs), f32) for _ in range(ACC)]
    arrived, leaving = order_of(OUT_ORDER, seq_count), order_of(BACK_ORDER, seq_count)
    for at, device in enumerate(arrived):
        for step in range(subs // 2):
            halves = []
            for sub in (2 * step, 2 * step + 1):
                base = at * (subs * group + 1) + sub * group
                from_row = at * per + (sub * 3 + 2) * group
                mixed = conv[base : base + group, :] * taken[from_row : from_row + group, :]
                out[leaving.index(device), sub * group : (sub + 1) * group, :] = mixed
                halves.append(mixed)
            hi, lo = split(jnp.concatenate(halves, 1))
            offset = (device * subs + 2 * step) * LANES
            member = jnp.where(
                (past_start >= jnp.int16(-offset)) & (to_end >= jnp.int16(offset)), one, zero
            )
            which = (at * (subs // 2) + step) % ACC
            sums[which] = sums[which] + mm(jnp.concatenate([hi, lo], 0), member)
    acc = sum(sums[1:], sums[0])
    pooled = (acc[:group] + acc[group:]) / sizes[:group, :]
    pooled = jnp.concatenate([pooled, jnp.zeros((LANES - group, segs), f32)], 0).T
    shift = lax.rem(place_in(arrived), LANES // group) * group
    pooled = pltpu.roll(pooled, shift, 1)
    for at, device in enumerate(leaving):
        out[at, subs * group :, :] = pooled[device * owned : (device + 1) * owned, :]


def back_kernel(taken, mixed, pooled, turned, summed, sems, *, seq_count, group, subs):
    channels = seq_count * group
    leaving = order_of(BACK_ORDER, seq_count)
    holder = [leaving.index(device) for device in order_of(OUT_ORDER, seq_count)]
    copies = []
    per_lane = LANES // group
    for half in range(channels // LANES):
        total = taken[holder[half * per_lane], subs * group :, :]
        for at in holder[half * per_lane + 1 : (half + 1) * per_lane]:
            total = total + taken[at, subs * group :, :]
        summed[:, half * LANES : (half + 1) * LANES] = total
    copies.append(pltpu.make_async_copy(summed, pooled, sems.at[subs]))
    copies[-1].start()
    for sub in range(subs):
        block = jnp.concatenate([taken[at, sub * group : (sub + 1) * group, :] for at in holder], 0)
        turned[sub] = block.T
        rows = pl.ds(sub * LANES, LANES)
        copies.append(pltpu.make_async_copy(turned.at[sub], mixed.at[rows, :], sems.at[sub]))
        copies[-1].start()
    for copy in copies:
        copy.wait()


def in_vmem(value):
    return pltpu.with_memory_space_constraint(value, pltpu.VMEM)


def on_device(signal, filter_taps, out_gate, skip_gain, lengths, row_of_segment):
    seq_count = lax.axis_size("seq")
    block_rows, channels = signal.shape
    group = channels // seq_count
    subs = block_rows // LANES
    segs = lengths.shape[0]
    owned = segs // seq_count
    sizes = dict(seq_count=seq_count, group=group, subs=subs)
    anywhere = pl.BlockSpec(memory_space=pltpu.HBM)
    consts = jnp.asarray(tables(seq_count, subs))
    sent, bounds, row_sizes, table = pl.pallas_call(
        functools.partial(turn_kernel, **sizes),
        in_specs=[anywhere] * 7,
        out_shape=(
            pltpu.VMEM((seq_count, 3 * subs * group, LANES), f32),
            pltpu.VMEM((2 * group, segs), f32),
            pltpu.VMEM((2 * group, segs), f32),
            pltpu.VMEM(consts.shape, bf16),
        ),
        scratch_shapes=[
            pltpu.VMEM((3, subs * LANES, channels), f32),
            pltpu.VMEM((1, channels), f32),
            pltpu.VMEM((2, 1, segs), jnp.int32),
            pltpu.SemaphoreType.DMA((3 * subs,)),
            pltpu.SemaphoreType.DMA((4,)),
        ],
        interpret=INTERPRET,
        name="turn",
        compiler_params=pltpu.CompilerParams(vmem_limit_bytes=VMEM_LIMIT),
    )(
        *(
            pltpu.with_memory_space_constraint(value, pltpu.HBM)
            for value in (
                signal,
                filter_taps,
                out_gate,
                skip_gain.reshape(1, channels),
                lengths.reshape(1, segs),
                row_of_segment.reshape(1, segs),
                consts,
            )
        )
    )
    taken = exchange(sent, order_of(OUT_ORDER, seq_count))
    taken = in_vmem(taken.reshape(seq_count * 3 * subs * group, LANES))
    mixed_sent = pl.pallas_call(
        functools.partial(conv_kernel, **sizes),
        out_shape=pltpu.VMEM((seq_count, subs * group + owned, LANES), f32),
        scratch_shapes=[
            pltpu.VMEM((seq_count * (subs * group + 1), LANES), f32),
            pltpu.VMEM((2 * group * seq_count * subs, 4 * LANES), bf16),
            pltpu.VMEM((group * seq_count * subs, 4 * LANES), bf16),
            pltpu.VMEM((2 * group * seq_count * subs, 2 * LANES), bf16),
            pltpu.VMEM((seq_count * (2 * subs * group + 1), LANES), f32),
        ],
        interpret=INTERPRET,
        name="conv",
        compiler_params=pltpu.CompilerParams(vmem_limit_bytes=VMEM_LIMIT),
    )(taken, in_vmem(bounds), in_vmem(row_sizes), in_vmem(table))
    back = exchange(mixed_sent, order_of(BACK_ORDER, seq_count))
    back = in_vmem(back)
    return pl.pallas_call(
        functools.partial(back_kernel, **sizes),
        out_shape=(
            jax.ShapeDtypeStruct((block_rows, channels), f32),
            jax.ShapeDtypeStruct((owned, channels), f32),
        ),
        out_specs=(pl.BlockSpec(memory_space=pltpu.HBM), pl.BlockSpec(memory_space=pltpu.HBM)),
        scratch_shapes=[
            pltpu.VMEM((subs, LANES, channels), f32),
            pltpu.VMEM((owned, channels), f32),
            pltpu.SemaphoreType.DMA((subs + 1,)),
        ],
        interpret=INTERPRET,
        name="back",
        compiler_params=pltpu.CompilerParams(vmem_limit_bytes=VMEM_LIMIT),
    )(back)


def solution(mesh):
    placed = (P("seq", "chan"), P("seq", "chan"), P("seq", "chan"), P("chan"), P(), P())
    return jax.shard_map(
        on_device,
        mesh=mesh,
        in_specs=placed,
        out_specs=(P("seq", "chan"), P("seq", "chan")),
        check_vma=False,
    )
```
